256 devices in a mesh: seq: 32 (over y, x, core), rep: 8 (over z).
Axes of the slice: x: 4, y: 4, z: 8, core: 2. Of those that a mesh axis runs over, the one named last changes fastest.
Arguments:
- tokens: bfloat16 [8, 4096, 1024], P('rep', 'seq'), may hold values from -16 to 16
- cotangent: bfloat16 [8, 4096, 1024], P('rep', 'seq'), may hold values from -6 to 6
- weights: bfloat16 [4, 1024, 512], replicated, may hold values from -0.1875 to 0.1875
- neighbour_lists: int32 [8, 32, 27], P('rep'), may hold values from 0 to 31, as said below
- neighbour_counts: int32 [8, 32], P('rep'), may hold values from 1 to 27, as said below
Outputs:
- output: bfloat16 [8, 4096, 1024], P('rep', 'seq')
- d_inputs: bfloat16 [8, 4096, 1024], P('rep', 'seq')
- weight_grads: float32 [4, 1024, 512], P(None, ('seq', 'rep'))
The draws below stay inside these ranges and needn't reach their ends.
Inputs may be any that keep to these rules, and one draw needn't show every extreme that they name: `neighbour_lists`: slot 0 of every list is the block itself; the live slots of a list name distinct blocks of the same replica's slab; dead slots hold the block's own position. `neighbour_counts`: in each replica some block has min(27, 32) live slots.
All inputs are finite; a program needn't handle non-finite values.
Results may differ from the reference program's by a relative error of at most 0.023.
The reference program's roundings to bfloat16 on the way count: a program that leaves them out, or rounds other values in their place, can miss the bound.
Values may be sent and summed in bfloat16 or wider, within the bound.
No kernel may reach another device: no remote copies, remote signals or barrier semaphores. Data moves between devices by JAX's collectives and lax.ppermute only.
A program may use at most 128 MiB of HBM per device.

```python
import math
import jax
import jax.numpy as jnp
from jax import lax

D = 1024
HEADS = 8
HEAD_DIM = 64
BLOCK = 128
MAXN = 27
HD = 512
BLOCKS = 32
TOKENS = 4096
N_REP = 8


def neighbour_tables(key):
    key = jax.random.fold_in(key, 11)
    key_rank, key_count, key_pick = jax.random.split(key, 3)
    capacity = min(MAXN, BLOCKS)
    raw_bits = jax.random.randint(key_rank, (N_REP, BLOCKS, BLOCKS), 0, 1 << 20)
    block_ids = jnp.arange(BLOCKS, dtype=jnp.int32)
    ranked = raw_bits * BLOCKS + block_ids[None, None, :]
    ranked = jnp.where(block_ids[None, :, None] == block_ids[None, None, :], -1, ranked)
    ranking = jnp.argsort(ranked, axis=-1, stable=True).astype(jnp.int32)
    own_ids = jnp.broadcast_to(block_ids[None, :, None], (N_REP, BLOCKS, MAXN)).astype(jnp.int32)
    picked = jnp.concatenate([ranking[:, :, :capacity], own_ids[:, :, capacity:]], axis=-1)
    counts = jax.random.randint(key_count, (N_REP, BLOCKS), 1, capacity + 1)
    chosen = jax.random.randint(key_pick, (N_REP, 1), 0, BLOCKS)
    counts = jnp.where(block_ids[None, :] == chosen, capacity, counts).astype(jnp.int32)
    slot_ids = jnp.arange(MAXN, dtype=jnp.int32)
    lists = jnp.where(slot_ids[None, None, :] < counts[:, :, None], picked, own_ids).astype(jnp.int32)
    return (lists, counts)


def draw_neighbour_lists(key, part):
    return neighbour_tables(key)[0]


def draw_neighbour_counts(key, part):
    return neighbour_tables(key)[1]


def draw_tokens(key, part):
    dims_all = (N_REP, TOKENS, D)
    key_base = jax.random.fold_in(key, 0)
    return jnp.clip(jax.random.normal(key_base, dims_all, jnp.float32), -4.0, 4.0).astype(jnp.bfloat16)


def strengthened(array, own_key, source, target, parts, factor):
    def block_of(position):
        return (jnp.arange(array.shape[position]) // (array.shape[position] // parts)).reshape((-1,) + (1,) * (array.ndim - 1 - position))

    first = jax.random.permutation(own_key, parts)[block_of(target)]
    second = (block_of(target) + parts // 2) % parts
    return jnp.where((block_of(source) == first) | (block_of(source) == second), factor * array, array)


def steps_of(own_key, dims, cuts, low, largest):
    loudness, own = 1.0, jax.random.fold_in(own_key, 6)
    for dim, parts in cuts:
        heights = jnp.exp(jax.random.uniform(jax.random.fold_in(own, dim), (parts,), jnp.float32, low / len(cuts), largest / len(cuts)))
        loudness = loudness * jnp.repeat(heights, dims[dim] // parts).reshape([-1 if axis == dim else 1 for axis in range(len(dims))])
    return loudness


def centred(rng, shape, width, bound, shards=(), held_as=jnp.bfloat16):
    result = width * jax.random.normal(rng, shape, jnp.float32)
    if shards:
        result = result * steps_of(rng, shape, shards, -0.22, 0.18)
    return jnp.clip(result, -bound, bound).astype(held_as)


def bell_draw_with(key, dims, scale, limit, cuts, heavy, held_as=jnp.bfloat16):
    result = scale * jax.random.normal(key, dims, jnp.float32)
    if cuts:
        result = result * steps_of(key, dims, cuts, -0.22, 0.18)
    return jnp.clip(strengthened(result, jax.random.fold_in(key, 3), *heavy), -limit, limit).astype(held_as)


def setup_inputs(seed: int = 0) -> dict:
    splits = jax.random.split(jax.random.key(seed), 6)
    return {
        "tokens": draw_tokens(jax.random.fold_in(splits[5], 71), 0),
        "cotangent": bell_draw_with(splits[1], (N_REP, TOKENS, D), 1.0, 6.0, ((0, 8), (1, 32)), (1, 2, 32, 2.75)),
        "weights": centred(splits[2], (4, D, HD), D ** -0.5, 0.1875),
        "neighbour_lists": draw_neighbour_lists(jax.random.fold_in(splits[5], 71), 0),
        "neighbour_counts": draw_neighbour_counts(jax.random.fold_in(splits[5], 71), 0),
    }


def scores_of(query_block, slot_keys, live_count):
    score_scale = 1.0 / math.sqrt(HEAD_DIM)
    raw_scores = jnp.einsum('qhd,khd->hqk', query_block.astype(jnp.float32), slot_keys.astype(jnp.float32)) * score_scale
    live_cols = jnp.arange(slot_keys.shape[0]) // BLOCK < live_count
    return jnp.where(live_cols[None, None, :], raw_scores, -1e+30)

def one_replica(inputs, upstream, weights, lists, counts):
    score_scale = 1.0 / math.sqrt(HEAD_DIM)
    w_query, w_key, w_value, w_out = (weights[0], weights[1], weights[2], weights[3])
    shape_heads = (BLOCKS, BLOCK, HEADS, HEAD_DIM)
    queries = jnp.dot(inputs, w_query, preferred_element_type=jnp.float32).astype(jnp.bfloat16).reshape(shape_heads)
    key_rows = jnp.dot(inputs, w_key, preferred_element_type=jnp.float32).astype(jnp.bfloat16).reshape(shape_heads)
    value_rows = jnp.dot(inputs, w_value, preferred_element_type=jnp.float32).astype(jnp.bfloat16).reshape(shape_heads)

    def forward_block(block_data):
        query_block, slot_list, live_count = block_data
        slot_keys = key_rows[slot_list].reshape(MAXN * BLOCK, HEADS, HEAD_DIM)
        slot_values = value_rows[slot_list].reshape(MAXN * BLOCK, HEADS, HEAD_DIM)
        scores = scores_of(query_block, slot_keys, live_count)
        row_max = lax.optimization_barrier(jnp.max(scores, axis=-1))
        exponent = jnp.exp(scores - row_max[..., None])
        totals = lax.optimization_barrier(jnp.sum(exponent, axis=-1))
        mixed = jnp.einsum('hqk,khd->qhd', exponent.astype(jnp.bfloat16).astype(jnp.float32), slot_values.astype(jnp.float32))
        attended = (mixed / jnp.transpose(totals)[:, :, None]).astype(jnp.bfloat16)
        return (attended, row_max, totals)
    attended, row_max, totals = lax.map(forward_block, (queries, lists, counts))
    attended_flat = attended.reshape(TOKENS, HD)
    output = lax.dot_general(attended_flat, w_out, (((1,), (1,)), ((), ())), preferred_element_type=jnp.float32).astype(jnp.bfloat16)
    d_attended = jnp.dot(upstream, w_out, preferred_element_type=jnp.float32).astype(jnp.bfloat16)
    grad_out = lax.dot_general(upstream, attended_flat, (((0,), (0,)), ((), ())), preferred_element_type=jnp.float32)
    d_heads = d_attended.reshape(shape_heads)
    row_delta = lax.optimization_barrier(jnp.sum(d_heads.astype(jnp.float32) * attended.astype(jnp.float32), axis=-1))

    def backward_block(carry, block_data):
        key_acc, value_acc = carry
        query_block, d_block, delta_block, max_block, total_block, slot_list, live_count = block_data
        slot_keys = key_rows[slot_list].reshape(MAXN * BLOCK, HEADS, HEAD_DIM)
        slot_values = value_rows[slot_list].reshape(MAXN * BLOCK, HEADS, HEAD_DIM)
        scores = scores_of(query_block, slot_keys, live_count)
        normed = jnp.exp(scores - max_block[..., None]) / total_block[..., None]
        d_probs = jnp.einsum('qhd,khd->hqk', d_block.astype(jnp.float32), slot_values.astype(jnp.float32))
        d_scores = (normed * (d_probs - jnp.transpose(delta_block)[:, :, None])).astype(jnp.bfloat16)
        d_query = (jnp.einsum('hqk,khd->qhd', d_scores.astype(jnp.float32), slot_keys.astype(jnp.float32)) * score_scale).astype(jnp.bfloat16)
        key_terms = jnp.einsum('hqk,qhd->khd', d_scores.astype(jnp.float32), query_block.astype(jnp.float32)) * score_scale
        value_terms = jnp.einsum('hqk,qhd->khd', normed.astype(jnp.bfloat16).astype(jnp.float32), d_block.astype(jnp.float32))
        key_acc = key_acc.at[slot_list].add(key_terms.reshape(MAXN, BLOCK, HEADS, HEAD_DIM))
        value_acc = value_acc.at[slot_list].add(value_terms.reshape(MAXN, BLOCK, HEADS, HEAD_DIM))
        return ((key_acc, value_acc), d_query)
    zeros_acc = jnp.zeros(shape_heads, jnp.float32)
    (key_sum, value_sum), d_queries = lax.scan(backward_block, (zeros_acc, zeros_acc), (queries, d_heads, row_delta, row_max, totals, lists, counts))
    stacked = jnp.concatenate([d_queries.reshape(TOKENS, HD), key_sum.astype(jnp.bfloat16).reshape(TOKENS, HD), value_sum.astype(jnp.bfloat16).reshape(TOKENS, HD)], axis=1)
    w_joined = jnp.concatenate([w_query, w_key, w_value], axis=1)
    d_inputs = lax.dot_general(stacked, w_joined, (((1,), (1,)), ((), ())), preferred_element_type=jnp.float32).astype(jnp.bfloat16)
    grad_joined = lax.dot_general(inputs, stacked, (((0,), (0,)), ((), ())), preferred_element_type=jnp.float32)
    grad_three = jnp.transpose(grad_joined.reshape(D, 3, HD), (1, 0, 2))
    grads = jnp.concatenate([grad_three, grad_out[None]], axis=0)
    return (output, d_inputs, grads)

def reference(tokens, cotangent, weights, neighbour_lists, neighbour_counts):
    outputs_all = []
    inputs_grad_all = []
    grad_total = jnp.zeros((4, D, HD), jnp.float32)
    for replica in range(N_REP):
        output, d_inputs, grads = one_replica(tokens[replica], cotangent[replica], weights, neighbour_lists[replica], neighbour_counts[replica])
        outputs_all.append(output)
        inputs_grad_all.append(d_inputs)
        grad_total = grad_total + grads
    return (jnp.stack(outputs_all), jnp.stack(inputs_grad_all), grad_total)
```

```python
import functools

import jax
import jax.numpy as jnp
from jax import lax
from jax.experimental import pallas as pl
from jax.experimental.pallas import tpu as pltpu
from jax.sharding import Mesh, PartitionSpec as P

HEADS = 8
HEAD_DIM = 64
BLOCK = 128
MAXN = 27
GROUP = 4
SLOTS = 28
BF = jnp.bfloat16
F32 = jnp.float32
INTERPRET = False


def dot(a, b):
    return jnp.dot(a, b, preferred_element_type=F32)


def dot_t(a, b):
    return lax.dot_general(a, b, (((1,), (1,)), ((), ())), preferred_element_type=F32)


def vmem(count):
    return [pl.BlockSpec(memory_space=pltpu.VMEM) for _ in range(count)]


def project_kernel(tok_ref, cot_ref, w_ref, kv_ref, qd_ref, xt_ref, rows):
    step = pl.program_id(0)

    @pl.when(step < 3)
    def _():
        rows[step] = dot(tok_ref[...], w_ref[0]).astype(BF)

    @pl.when(step == 3)
    def _():
        rows[3] = dot(cot_ref[...], w_ref[0]).astype(BF)
        for head in range(HEADS):
            cols = slice(head * HEAD_DIM, (head + 1) * HEAD_DIM)
            scaled = (rows[0, :, cols].astype(F32) * 0.125).astype(BF)
            kv_ref[head] = jnp.concatenate([rows[1, :, cols], rows[2, :, cols]], axis=1)
            qd_ref[head] = jnp.concatenate([scaled, rows[3, :, cols]], axis=1)

    @pl.when(step == 0)
    def _():
        xt_ref[0] = tok_ref[...].T

    @pl.when(step == 1)
    def _():
        xt_ref[1] = cot_ref[...].T


def project(tok, cot, weights):
    rows, width = tok.shape
    whole = lambda step: (0, 0)
    whole3 = lambda step: (0, 0, 0)
    return pl.pallas_call(
        project_kernel,
        grid=(4,),
        in_specs=[
            pl.BlockSpec((rows, width), whole),
            pl.BlockSpec((rows, width), whole),
            pl.BlockSpec((1, width, HEADS * HEAD_DIM), lambda step: (step, 0, 0)),
        ],
        out_specs=[
            pl.BlockSpec((HEADS, rows, 128), whole3),
            pl.BlockSpec((HEADS, rows, 128), whole3),
            pl.BlockSpec((2, width, rows), whole3),
        ],
        out_shape=[
            jax.ShapeDtypeStruct((HEADS, rows, 128), BF),
            jax.ShapeDtypeStruct((HEADS, rows, 128), BF),
            jax.ShapeDtypeStruct((2, width, rows), BF),
        ],
        scratch_shapes=[pltpu.VMEM((4, rows, HEADS * HEAD_DIM), BF)],
        interpret=INTERPRET,
        name="project",
    )(tok, cot, weights)


def attend_kernel(
    lists_ref, counts_ref, group_ref,
    qd_ref, kv0, kv1, kv2, kv3,
    y_ref, out0, out1, out2, out3,
    kvs, kvt, acc, s_scr, p_scr,
):
    step = pl.program_id(0)
    group = group_ref[0]
    block = group * 8 + step

    @pl.when(step == 0)
    def _():
        for part, ref in enumerate((kv0, kv1, kv2, kv3)):
            for idx in range(8):
                piece = ref[idx]
                kvs[part * 8 + idx] = piece
                kvt[part * 8 + idx] = piece.T
        acc[...] = jnp.zeros_like(acc)

    count = counts_ref[block]
    trips = (count + GROUP - 1) // GROUP

    def place(slot):
        raw = lists_ref[block, jnp.minimum(slot, MAXN - 1)]
        raw = jnp.where(slot < count, raw, block)
        return lax.rem(group - raw // 8 + 4, 4) * 8 + lax.rem(raw, 8)

    qd = qd_ref[0]
    qdt = qd.T
    upper = lax.broadcasted_iota(jnp.int32, (128, 128), 0) < HEAD_DIM
    left = lax.broadcasted_iota(jnp.int32, (128, 128), 1) < HEAD_DIM
    zero = jnp.zeros((128, 128), BF)
    w_in = jnp.concatenate([jnp.where(upper, qdt, zero), jnp.where(upper, zero, qdt)], axis=1)
    w_back = jnp.concatenate([jnp.where(left, qd, zero), jnp.where(left, zero, qd)], axis=0)
    span = GROUP * 128

    def scores(trip, top):
        stack = jnp.concatenate(
            [kvs[place(trip * GROUP + i)] for i in range(GROUP)], axis=0
        )
        both = dot(stack, w_in)
        base = pl.multiple_of(trip * span, span)
        s_scr[pl.ds(base, span), :] = both[:, :128]
        p_scr[pl.ds(base, span), :] = both[:, 128:]
        return jnp.maximum(top, jnp.max(both[:, :128].reshape(span // 8, 8, 128), axis=0))

    top = lax.fori_loop(0, trips, scores, jnp.full((8, 128), -3e38, F32))
    row_max = jnp.max(top, axis=0, keepdims=True)

    def mix(trip, carry):
        total, mixed = carry
        base = pl.multiple_of(trip * span, span)
        parts, values = [], []
        for i in range(GROUP):
            slot = trip * GROUP + i
            shift = jnp.where(slot < count, row_max, 1e30)
            e = jnp.exp(s_scr[pl.ds(base + i * 128, 128), :] - shift)
            s_scr[pl.ds(base + i * 128, 128), :] = e
            total = total + jnp.sum(e.reshape(16, 8, 128), axis=0)
            parts.append(e.astype(BF))
            values.append(kvt[place(slot), HEAD_DIM:, :])
        mixed = mixed + dot(jnp.concatenate(values, axis=1), jnp.concatenate(parts, axis=0))
        return total, mixed

    total, mixed = lax.fori_loop(
        0, trips, mix, (jnp.zeros((8, 128), F32), jnp.zeros((HEAD_DIM, 128), F32))
    )
    inverse = 1.0 / jnp.sum(total, axis=0, keepdims=True)
    attended = (mixed * inverse).astype(BF)
    delta = jnp.sum(
        qdt[HEAD_DIM:, :].astype(F32) * attended.astype(F32), axis=0, keepdims=True
    )

    def back(trip, dq):
        base = pl.multiple_of(trip * span, span)
        dss, pairs, keys, places = [], [], [], []
        for i in range(GROUP):
            rows = pl.ds(base + i * 128, 128)
            normed = s_scr[rows, :] * inverse
            ds = (normed * (p_scr[rows, :] - delta)).astype(BF)
            dss.append(ds)
            pairs.append(jnp.concatenate([ds, normed.astype(BF)], axis=1))
            where = place(trip * GROUP + i)
            places.append(where)
            keys.append(kvt[where, :HEAD_DIM, :])
        dq = dq + dot(jnp.concatenate(keys, axis=1), jnp.concatenate(dss, axis=0))
        grads = dot(jnp.concatenate(pairs, axis=0), w_back)
        for i in range(GROUP):
            acc[places[i]] += grads[i * 128 : (i + 1) * 128]
        return dq

    dq = lax.fori_loop(0, trips, back, jnp.zeros((HEAD_DIM, 128), F32))
    y_ref[0] = jnp.concatenate([dq * 0.125, attended.astype(F32)], axis=0).T.astype(BF)

    @pl.when(step == 7)
    def _():
        out0[...] = acc[0:8]
        for part, ref in enumerate((out1, out2, out3)):
            ref[...] = acc[8 * (part + 1) : 8 * (part + 2)].astype(BF)


def attend(lists, counts, group, qd, parts):
    whole3 = lambda step, *_: (0, 0, 0)
    piece = pl.BlockSpec((8, 128, 128), whole3)
    each = pl.BlockSpec((1, 128, 128), lambda step, *_: (step, 0, 0))
    shape = lambda dtype: jax.ShapeDtypeStruct((8, 128, 128), dtype)
    return pl.pallas_call(
        attend_kernel,
        grid_spec=pltpu.PrefetchScalarGridSpec(
            num_scalar_prefetch=3,
            grid=(8,),
            in_specs=[each] + [piece] * 4,
            out_specs=[each] + [piece] * 4,
            scratch_shapes=[
                pltpu.VMEM((32, 128, 128), BF),
                pltpu.VMEM((32, 128, 128), BF),
                pltpu.VMEM((32, 128, 128), F32),
                pltpu.VMEM((SLOTS * 128, 128), F32),
                pltpu.VMEM((SLOTS * 128, 128), F32),
            ],
        ),
        out_shape=[shape(BF), shape(F32), shape(BF), shape(BF), shape(BF)],
        cost_estimate=pl.CostEstimate(
            flops=30_000_000_000, bytes_accessed=4_000_000, transcendentals=4_000_000
        ),
        interpret=INTERPRET,
        name="attend",
    )(lists, counts, group, qd, *parts)


def ordered(y_ref, place):
    pieces = []
    for flip in range(2):
        for hop in (0, 1, 3, 2):
            source = lax.rem(place - 2 * hop + 8, 8)
            if flip:
                source = source + 1 - 2 * lax.rem(source, 2)
            pieces.append(y_ref[source])
    return jnp.concatenate(pieces, axis=0)


def inputs_of(x0, x1, x2, x3, far, which):
    return jnp.concatenate(
        [x0[which], x1[which], x2[which], x3[which]] + [far[i, which] for i in range(4)], axis=1
    )


def first_grads_kernel(place_ref, y_ref, x0, x1, x2, x3, far, out_ref):
    y = ordered(y_ref, place_ref[0])
    tok = dot(inputs_of(x0, x1, x2, x3, far, 0), y)
    cot = dot(inputs_of(x0, x1, x2, x3, far, 1), y)
    left = lax.broadcasted_iota(jnp.int32, tok.shape, 1) < HEAD_DIM
    out_ref[...] = jnp.where(left, tok, cot).astype(out_ref.dtype)


def second_grads_kernel(place_ref, part0, part1, part2, part3, x0, x1, x2, x3, far, out_ref, y_ref):
    y_ref[...] = (
        part0[...]
        + part1[...].astype(F32)
        + part2[...].astype(F32)
        + part3[...].astype(F32)
    ).astype(BF)
    y = ordered(y_ref, place_ref[0])
    out_ref[...] = dot(inputs_of(x0, x1, x2, x3, far, 0), y).astype(out_ref.dtype)


def smem():
    return pl.BlockSpec(memory_space=pltpu.SMEM)


def first_grads(place, y, xs, width):
    return pl.pallas_call(
        first_grads_kernel,
        in_specs=[smem()] + vmem(6),
        out_specs=pl.BlockSpec(memory_space=pltpu.VMEM),
        out_shape=jax.ShapeDtypeStruct((width, 128), BF),
        cost_estimate=pl.CostEstimate(
            flops=2_000_000_000, bytes_accessed=4_000_000, transcendentals=0
        ),
        interpret=INTERPRET,
        name="first_grads",
    )(place, y, *xs)


def second_grads(place, parts, xs, width):
    return pl.pallas_call(
        second_grads_kernel,
        in_specs=[smem()] + vmem(9),
        out_specs=vmem(2),
        out_shape=[
            jax.ShapeDtypeStruct((width, 128), BF),
            jax.ShapeDtypeStruct((8, 128, 128), BF),
        ],
        cost_estimate=pl.CostEstimate(
            flops=2_000_000_000, bytes_accessed=4_000_000, transcendentals=0
        ),
        interpret=INTERPRET,
        name="second_grads",
    )(place, *parts, *xs)


def halves(y_ref):
    first = jnp.concatenate([y_ref[h, :, :HEAD_DIM] for h in range(HEADS)], axis=1)
    second = jnp.concatenate([y_ref[h, :, HEAD_DIM:] for h in range(HEADS)], axis=1)
    return first, second


def output_kernel(y_ref, wq_ref, wo_ref, out_ref, part_ref):
    dq, attended = halves(y_ref)
    out_ref[...] = dot_t(attended, wo_ref[0]).astype(BF)
    part_ref[...] = dot_t(dq, wq_ref[0])


def inputs_kernel(y_ref, part_ref, wk_ref, wv_ref, out_ref):
    dk, dv = halves(y_ref)
    out_ref[...] = (part_ref[...] + dot_t(dk, wk_ref[0]) + dot_t(dv, wv_ref[0])).astype(BF)


def last_products(kernel, name, y, extra, weights, picks, outs):
    rows, width = y.shape[1], weights.shape[1]
    wide = pl.BlockSpec((rows, width), lambda step: (0, 0))
    pick = lambda m: pl.BlockSpec((1, width, HEADS * HEAD_DIM), lambda step: (m, 0, 0))
    return pl.pallas_call(
        kernel,
        grid=(1,),
        in_specs=[pl.BlockSpec(y.shape, lambda step: (0, 0, 0))]
        + [wide for _ in extra]
        + [pick(m) for m in picks],
        out_specs=[wide for _ in outs],
        out_shape=[jax.ShapeDtypeStruct((rows, width), dtype) for dtype in outs],
        cost_estimate=pl.CostEstimate(
            flops=500_000_000, bytes_accessed=4_000_000, transcendentals=0
        ),
        interpret=INTERPRET,
        name=name,
    )(y, *extra, *[weights for _ in picks])


def reduced(received, rows):
    sums = received.astype(F32).reshape(4, 8, -1, rows, 2, HEAD_DIM).sum(axis=(0, 2))
    return jnp.transpose(sums, (2, 1, 0, 3)).reshape(2, rows, HEADS * HEAD_DIM)


def shift(axis_size, hop):
    return [(i, (i + hop) % axis_size) for i in range(axis_size)]


def body(tokens, cotangent, weights, neighbour_lists, neighbour_counts):
    width = tokens.shape[2]
    group = lax.axis_index("row").astype(jnp.int32).reshape(1)
    place = lax.axis_index("head").astype(jnp.int32).reshape(1)
    swap = lambda array: lax.all_to_all(array, "head", 0, 0, tiled=True)

    kv, qd, xt = project(tokens[0], cotangent[0], weights)
    kv = swap(kv)
    qd, xt, kv = lax.optimization_barrier((qd, xt, kv))
    kvs = [kv] + [lax.ppermute(kv, "row", shift(4, hop)) for hop in (1, 2, 3)]
    qd = swap(qd)
    near = [xt] + [lax.ppermute(xt, "head", shift(8, 2 * hop)) for hop in (1, 3, 2)]
    far = lax.ppermute(jnp.stack(near), "head", [(i, i ^ 1) for i in range(8)])
    xs = near + [far]

    y, part0, part1, part2, part3 = attend(
        neighbour_lists[0], neighbour_counts[0], group, qd, kvs
    )
    parts = [part0] + [
        lax.ppermute(part, "row", shift(4, -hop))
        for hop, part in ((1, part1), (2, part2), (3, part3))
    ]
    home = swap(y)
    output, partial = last_products(
        output_kernel, "output", home, (), weights, (0, 3), (BF, F32)
    )
    every = ("row", "head", "rep")
    devices = 32 * lax.axis_size("rep")
    rows = width // devices
    scatter = lambda grads: reduced(
        lax.all_to_all(grads.reshape(devices, rows, 128), every, 0, 0, tiled=True), rows
    )
    first = scatter(first_grads(place, y, xs, width))
    grads, y2 = second_grads(place, parts, xs, width)
    second = scatter(grads)
    (d_inputs,) = last_products(
        inputs_kernel, "d_inputs", swap(y2), (partial,), weights, (1, 2), (BF,)
    )
    summed = jnp.concatenate([first[:1], second, first[1:]], axis=0)
    return (output[None], d_inputs[None], summed)


def solution(mesh):
    grid = Mesh(mesh.devices.reshape(4, 8, mesh.devices.shape[1]), ("row", "head", "rep"))
    seq = ("row", "head")
    return jax.shard_map(
        body,
        mesh=grid,
        in_specs=(
            P("rep", seq, None),
            P("rep", seq, None),
            P(),
            P("rep", None, None),
            P("rep", None),
        ),
        out_specs=(
            P("rep", seq, None),
            P("rep", seq, None),
            P(None, ("row", "head", "rep"), None),
        ),
        check_vma=False,
    )
```

```python
import functools

import jax
import jax.numpy as jnp
from jax import lax
from jax.experimental import pallas as pl
from jax.experimental.pallas import tpu as pltpu
from jax.sharding import Mesh, PartitionSpec as P

HEADS = 8
HEAD_DIM = 64
BLOCK = 128
MAXN = 27
GROUP = 4
SLOTS = 28
BF = jnp.bfloat16
F32 = jnp.float32
INTERPRET = False


def dot(a, b):
    return jnp.dot(a, b, preferred_element_type=F32)


def dot_t(a, b):
    return lax.dot_general(a, b, (((1,), (1,)), ((), ())), preferred_element_type=F32)


def grant(mib):
    return pltpu.CompilerParams(vmem_limit_bytes=mib << 20)


def vmem(count):
    return [pl.BlockSpec(memory_space=pltpu.VMEM) for _ in range(count)]


def project_kernel(tok_ref, cot_ref, w_ref, kv_ref, qd_ref, xt_ref, rows):
    step = pl.program_id(0)

    @pl.when(step < 3)
    def _():
        rows[step] = dot(tok_ref[...], w_ref[0]).astype(BF)

    @pl.when(step == 3)
    def _():
        rows[3] = dot(cot_ref[...], w_ref[0]).astype(BF)
        for head in range(HEADS):
            cols = slice(head * HEAD_DIM, (head + 1) * HEAD_DIM)
            scaled = (rows[0, :, cols].astype(F32) * 0.125).astype(BF)
            kv_ref[head] = jnp.concatenate([rows[1, :, cols], rows[2, :, cols]], axis=1)
            qd_ref[head] = jnp.concatenate([scaled, rows[3, :, cols]], axis=1)

    @pl.when(step == 0)
    def _():
        xt_ref[0] = tok_ref[...].T

    @pl.when(step == 1)
    def _():
        xt_ref[1] = cot_ref[...].T


def project(tok, cot, weights):
    rows, width = tok.shape
    whole = lambda step: (0, 0)
    whole3 = lambda step: (0, 0, 0)
    return pl.pallas_call(
        project_kernel,
        grid=(4,),
        in_specs=[
            pl.BlockSpec((rows, width), whole),
            pl.BlockSpec((rows, width), whole),
            pl.BlockSpec((1, width, HEADS * HEAD_DIM), lambda step: (step, 0, 0)),
        ],
        out_specs=[
            pl.BlockSpec((HEADS, rows, 128), whole3),
            pl.BlockSpec((HEADS, rows, 128), whole3),
            pl.BlockSpec((2, width, rows), whole3),
        ],
        out_shape=[
            jax.ShapeDtypeStruct((HEADS, rows, 128), BF),
            jax.ShapeDtypeStruct((HEADS, rows, 128), BF),
            jax.ShapeDtypeStruct((2, width, rows), BF),
        ],
        scratch_shapes=[pltpu.VMEM((4, rows, HEADS * HEAD_DIM), BF)],
        compiler_params=grant(56),
        interpret=INTERPRET,
        name="project",
    )(tok, cot, weights)


def attend_kernel(
    lists_ref, counts_ref, group_ref,
    qd_ref, kv0, kv1, kv2, kv3,
    y_ref, out0, out1, out2, out3,
    kvs, kvt, acc, s_scr, p_scr, places,
):
    step = pl.program_id(0)
    group = group_ref[0]
    block = (step // 4) * 16 + (group // 2) * 8 + (step // 2 % 2) * 4 + group % 2 * 2 + step % 2

    @pl.when(step == 0)
    def _():
        for part, ref in enumerate((kv0, kv1, kv2, kv3)):
            for idx in range(8):
                piece = ref[idx]
                kvs[part * 8 + idx] = piece
                kvt[part * 8 + idx] = piece.T
        acc[...] = jnp.zeros_like(acc)

    count = counts_ref[block]
    trips = (count + GROUP - 1) // GROUP

    def place(slot):
        raw = lists_ref[block, jnp.minimum(slot, MAXN - 1)]
        raw = jnp.where(slot < count, raw, block)
        low = ((raw >> 3) & 1) * 2 + ((raw >> 1) & 1)
        where = (low ^ group) * 8 + ((raw >> 4) & 1) * 4 + ((raw >> 2) & 1) * 2 + (raw & 1)
        places[slot] = where
        return where

    qd = qd_ref[0]
    qdt = qd.T
    upper = lax.broadcasted_iota(jnp.int32, (128, 128), 0) < HEAD_DIM
    left = lax.broadcasted_iota(jnp.int32, (128, 128), 1) < HEAD_DIM
    zero = jnp.zeros((128, 128), BF)
    w_in = jnp.concatenate([jnp.where(upper, qdt, zero), jnp.where(upper, zero, qdt)], axis=1)
    w_back = jnp.concatenate([jnp.where(left, qd, zero), jnp.where(left, zero, qd)], axis=0)
    span = GROUP * 128

    def scores(trip, top):
        stack = jnp.concatenate(
            [kvs[place(trip * GROUP + i)] for i in range(GROUP)], axis=0
        )
        both = dot(stack, w_in)
        base = pl.multiple_of(trip * span, span)
        s_scr[pl.ds(base, span), :] = both[:, :128]
        p_scr[pl.ds(base, span), :] = both[:, 128:]
        return jnp.maximum(top, jnp.max(both[:, :128].reshape(span // 8, 8, 128), axis=0))

    top = lax.fori_loop(0, trips, scores, jnp.full((8, 128), -3e38, F32))
    row_max = jnp.max(top, axis=0, keepdims=True)

    def mix(trip, carry):
        total, mixed = carry
        base = pl.multiple_of(trip * span, span)
        parts, values = [], []
        for i in range(GROUP):
            slot = trip * GROUP + i
            shift = jnp.where(slot < count, row_max, 1e30)
            e = jnp.exp(s_scr[pl.ds(base + i * 128, 128), :] - shift)
            s_scr[pl.ds(base + i * 128, 128), :] = e
            total = total + jnp.sum(e.reshape(16, 8, 128), axis=0)
            parts.append(e.astype(BF))
            values.append(kvt[places[slot], HEAD_DIM:, :])
        mixed = mixed + dot(jnp.concatenate(values, axis=1), jnp.concatenate(parts, axis=0))
        return total, mixed

    total, mixed = lax.fori_loop(
        0, trips, mix, (jnp.zeros((8, 128), F32), jnp.zeros((HEAD_DIM, 128), F32))
    )
    inverse = 1.0 / jnp.sum(total, axis=0, keepdims=True)
    attended = (mixed * inverse).astype(BF)
    delta = jnp.sum(
        qdt[HEAD_DIM:, :].astype(F32) * attended.astype(F32), axis=0, keepdims=True
    )

    def back(trip, dq):
        base = pl.multiple_of(trip * span, span)
        dss, pairs, keys, targets = [], [], [], []
        for i in range(GROUP):
            rows = pl.ds(base + i * 128, 128)
            normed = s_scr[rows, :] * inverse
            ds = (normed * (p_scr[rows, :] - delta)).astype(BF)
            dss.append(ds)
            pairs.append(jnp.concatenate([ds, normed.astype(BF)], axis=1))
            where = places[trip * GROUP + i]
            targets.append(where)
            keys.append(kvt[where, :HEAD_DIM, :])
        dq = dq + dot(jnp.concatenate(keys, axis=1), jnp.concatenate(dss, axis=0))
        grads = dot(jnp.concatenate(pairs, axis=0), w_back)
        for i in range(GROUP):
            acc[targets[i]] += grads[i * 128 : (i + 1) * 128]
        return dq

    dq = lax.fori_loop(0, trips, back, jnp.zeros((HEAD_DIM, 128), F32))
    y_ref[0] = jnp.concatenate([dq * 0.125, attended.astype(F32)], axis=0).T.astype(BF)

    @pl.when(step == 7)
    def _():
        out0[...] = acc[0:8]
        for part, ref in enumerate((out1, out2, out3)):
            ref[...] = acc[8 * (part + 1) : 8 * (part + 2)].astype(BF)


def attend(lists, counts, group, qd, parts):
    whole3 = lambda step, *_: (0, 0, 0)
    piece = pl.BlockSpec((8, 128, 128), whole3)
    each = pl.BlockSpec((1, 128, 128), lambda step, *_: (step, 0, 0))
    shape = lambda dtype: jax.ShapeDtypeStruct((8, 128, 128), dtype)
    return pl.pallas_call(
        attend_kernel,
        grid_spec=pltpu.PrefetchScalarGridSpec(
            num_scalar_prefetch=3,
            grid=(8,),
            in_specs=[each] + [piece] * 4,
            out_specs=[each] + [piece] * 4,
            scratch_shapes=[
                pltpu.VMEM((32, 128, 128), BF),
                pltpu.VMEM((32, 128, 128), BF),
                pltpu.VMEM((32, 128, 128), F32),
                pltpu.VMEM((SLOTS * 128, 128), F32),
                pltpu.VMEM((SLOTS * 128, 128), F32),
                pltpu.SMEM((SLOTS,), jnp.int32),
            ],
        ),
        out_shape=[shape(BF), shape(F32), shape(BF), shape(BF), shape(BF)],
        cost_estimate=pl.CostEstimate(
            flops=30_000_000_000, bytes_accessed=4_000_000, transcendentals=4_000_000
        ),
        compiler_params=grant(28),
        interpret=INTERPRET,
        name="attend",
    )(lists, counts, group, qd, *parts)


def ordered(y_ref, place):
    return jnp.concatenate([y_ref[place ^ k] for k in (0, 2, 4, 6, 1, 3, 5, 7)], axis=0)


def deal(grads, group, scratch, outs):
    chunk = grads.shape[0] // 16
    for q in range(16):
        low, high = (q >> 2 & 1) * 2 + (q & 1), (q >> 3) * 2 + (q >> 1 & 1)
        scratch[low, high * chunk : (high + 1) * chunk, :] = grads[q * chunk : (q + 1) * chunk]
    outs[0][...] = scratch[group]
    for k in (1, 2, 3):
        outs[k][...] = scratch[group ^ k].astype(BF)


def first_grads_kernel(group_ref, place_ref, y_ref, *refs):
    xs, outs, scratch = refs[:8], refs[8:12], refs[12]
    y = ordered(y_ref, place_ref[0])
    tok = dot(jnp.concatenate([x[0] for x in xs], axis=1), y)
    cot = dot(jnp.concatenate([x[1] for x in xs], axis=1), y)
    left = lax.broadcasted_iota(jnp.int32, tok.shape, 1) < HEAD_DIM
    deal(jnp.where(left, tok, cot), group_ref[0], scratch, outs)


def second_grads_kernel(group_ref, place_ref, part0, part1, part2, part3, *refs):
    xs, outs, y_ref, scratch = refs[:8], refs[8:12], refs[12], refs[13]
    y_ref[...] = (
        part0[...]
        + part1[...].astype(F32)
        + part2[...].astype(F32)
        + part3[...].astype(F32)
    ).astype(BF)
    y = ordered(y_ref, place_ref[0])
    grads = dot(jnp.concatenate([x[0] for x in xs], axis=1), y)
    deal(grads, group_ref[0], scratch, outs)


def grads_call(kernel, name, group, place, operands, width, more):
    smem = pl.BlockSpec(memory_space=pltpu.SMEM)
    quarter = lambda dtype: jax.ShapeDtypeStruct((width // 4, 128), dtype)
    return pl.pallas_call(
        kernel,
        in_specs=[smem, smem] + vmem(len(operands)),
        out_specs=vmem(4 + len(more)),
        out_shape=[quarter(F32), quarter(BF), quarter(BF), quarter(BF)] + more,
        scratch_shapes=[pltpu.VMEM((4, width // 4, 128), F32)],
        cost_estimate=pl.CostEstimate(
            flops=2_000_000_000, bytes_accessed=4_000_000, transcendentals=0
        ),
        compiler_params=grant(16),
        interpret=INTERPRET,
        name=name,
    )(group, place, *operands)


def pair_kernel(*refs):
    total = lambda four: (
        four[0][...] + four[1][...].astype(F32) + four[2][...].astype(F32) + four[3][...].astype(F32)
    )
    first, second, out_ref = total(refs[0:4]), total(refs[4:8]), refs[8]
    rows = out_ref.shape[1] // 2
    for index in range(out_ref.shape[0]):
        mine = slice(index * rows, (index + 1) * rows)
        out_ref[index] = jnp.concatenate([first[mine], second[mine]], axis=0).astype(BF)


def gather_kernel(in_ref, out_ref):
    replicas, rows = in_ref.shape[0] // HEADS, in_ref.shape[1] // 2
    parts = []
    for head in range(HEADS):
        mine = in_ref[head * replicas : (head + 1) * replicas].astype(F32)
        parts.append(jnp.sum(mine, axis=0))
    for half, (near, far) in enumerate(((0, 3), (1, 2))):
        mine = slice(half * rows, (half + 1) * rows)
        out_ref[near] = jnp.concatenate([p[mine, :HEAD_DIM] for p in parts], axis=1)
        out_ref[far] = jnp.concatenate([p[mine, HEAD_DIM:] for p in parts], axis=1)


def small_call(kernel, name, operands, shape, dtype):
    return pl.pallas_call(
        kernel,
        in_specs=vmem(len(operands)),
        out_specs=pl.BlockSpec(memory_space=pltpu.VMEM),
        out_shape=jax.ShapeDtypeStruct(shape, dtype),
        compiler_params=grant(4),
        interpret=INTERPRET,
        name=name,
    )(*operands)


def halves(y_ref):
    first = jnp.concatenate([y_ref[h, :, :HEAD_DIM] for h in range(HEADS)], axis=1)
    second = jnp.concatenate([y_ref[h, :, HEAD_DIM:] for h in range(HEADS)], axis=1)
    return first, second


def output_kernel(y_ref, wq_ref, wo_ref, out_ref, part_ref):
    dq, attended = halves(y_ref)
    out_ref[...] = dot_t(attended, wo_ref[0]).astype(BF)
    part_ref[...] = dot_t(dq, wq_ref[0])


def inputs_kernel(y_ref, part_ref, wk_ref, wv_ref, out_ref):
    dk, dv = halves(y_ref)
    out_ref[...] = (part_ref[...] + dot_t(dk, wk_ref[0]) + dot_t(dv, wv_ref[0])).astype(BF)


def last_products(kernel, name, y, extra, weights, picks, outs):
    rows, width = y.shape[1], weights.shape[1]
    wide = pl.BlockSpec((rows, width), lambda step: (0, 0))
    pick = lambda m: pl.BlockSpec((1, width, HEADS * HEAD_DIM), lambda step: (m, 0, 0))
    return pl.pallas_call(
        kernel,
        grid=(1,),
        in_specs=[pl.BlockSpec(y.shape, lambda step: (0, 0, 0))]
        + [wide for _ in extra]
        + [pick(m) for m in picks],
        out_specs=[wide for _ in outs],
        out_shape=[jax.ShapeDtypeStruct((rows, width), dtype) for dtype in outs],
        cost_estimate=pl.CostEstimate(
            flops=500_000_000, bytes_accessed=4_000_000, transcendentals=0
        ),
        compiler_params=grant(12),
        interpret=INTERPRET,
        name=name,
    )(y, *extra, *[weights for _ in picks])


ROW = ("y_low", "x_low")
HEAD = ("y_high", "x_high", "core")
SEQ = ("y_high", "y_low", "x_high", "x_low", "core")


def across(array, axes, flip):
    size = 1 << len(axes)
    return lax.ppermute(array, axes, [(i, i ^ flip) for i in range(size)])


def body(tokens, cotangent, weights, neighbour_lists, neighbour_counts):
    width = tokens.shape[2]
    replicas = lax.axis_size("rep")
    rows = width // (32 * replicas)
    group = lax.axis_index(ROW).astype(jnp.int32).reshape(1)
    place = lax.axis_index(HEAD).astype(jnp.int32).reshape(1)
    swap = lambda array: lax.all_to_all(array, HEAD, 0, 0, tiled=True)

    kv, qd, xt = project(tokens[0], cotangent[0], weights)
    kv = swap(kv)
    qd, kv = lax.optimization_barrier((qd, kv))
    kvs = [kv] + [across(kv, ROW, k) for k in (1, 2, 3)]
    qd = swap(qd)
    xt, kvs = lax.optimization_barrier((xt, kvs))
    xs = [xt] + [across(xt, HEAD, k) for k in (2, 4, 6)]
    y, *parts = attend(neighbour_lists[0], neighbour_counts[0], group, qd, kvs)
    xs, y = lax.optimization_barrier((xs, y))
    xs = xs + [across(x, HEAD, 1) for x in xs]
    parts = [parts[0]] + [across(parts[k], ROW, k) for k in (1, 2, 3)]
    home = swap(y)
    output, partial = last_products(
        output_kernel, "output", home, (), weights, (0, 3), (BF, F32)
    )
    first = grads_call(first_grads_kernel, "first_grads", group, place, [y, *xs], width, [])
    first = [first[0]] + [across(first[k], ROW, k) for k in (1, 2, 3)]
    parts, first = lax.optimization_barrier((parts, first))
    *second, y2 = grads_call(
        second_grads_kernel, "second_grads", group, place, [*parts, *xs], width,
        [jax.ShapeDtypeStruct((8, 128, 128), BF)],
    )
    second = [second[0]] + [across(second[k], ROW, k) for k in (1, 2, 3)]
    home = swap(y2)
    (d_inputs,) = last_products(
        inputs_kernel, "d_inputs", home, (partial,), weights, (1, 2), (BF,)
    )
    terms = small_call(
        pair_kernel, "pair", [*first, *second], (8 * replicas, 2 * rows, 128), BF
    )
    terms = lax.all_to_all(terms, HEAD + ("rep",), 0, 0, tiled=True)
    summed = small_call(gather_kernel, "gather", [terms], (4, rows, HEADS * HEAD_DIM), F32)
    return (output[None], d_inputs[None], summed)


def solution(mesh):
    replicas = mesh.devices.shape[1]
    grid = Mesh(mesh.devices.reshape(2, 2, 2, 2, 2, replicas), SEQ + ("rep",))
    return jax.shard_map(
        body,
        mesh=grid,
        in_specs=(
            P("rep", SEQ, None),
            P("rep", SEQ, None),
            P(),
            P("rep", None, None),
            P("rep", None),
        ),
        out_specs=(
            P("rep", SEQ, None),
            P("rep", SEQ, None),
            P(None, SEQ + ("rep",), None),
        ),
        check_vma=False,
    )
```

```python
import jax
import jax.numpy as jnp
from jax import lax
from jax.experimental import pallas as pl
from jax.experimental.pallas import tpu as pltpu
from jax.sharding import Mesh, PartitionSpec as P


HEADS = 8
HEAD_DIM = 64
BLOCK = 128
MAXN = 27
GROUP = 4
SLOTS = 28
BF = jnp.bfloat16
F32 = jnp.float32
INTERPRET = False


def dot(a, b):
    return jnp.dot(a, b, preferred_element_type=F32)


def dot_t(a, b):
    return lax.dot_general(a, b, (((1,), (1,)), ((), ())), preferred_element_type=F32)


def grant(mib):
    return pltpu.CompilerParams(vmem_limit_bytes=mib << 20)


def vmem(count):
    return [pl.BlockSpec(memory_space=pltpu.VMEM) for _ in range(count)]


def position(high, low):
    return (high // 4) * 16 + (low // 2) * 8 + (high // 2 % 2) * 4 + (low % 2) * 2 + high % 2


def project_kernel(tok_ref, cot_ref, w_ref, kv_ref, qd_ref, xt_ref, rows):
    step = pl.program_id(0)

    @pl.when(step < 3)
    def _():
        rows[step] = dot(tok_ref[...], w_ref[0]).astype(BF)

    @pl.when(step == 3)
    def _():
        rows[3] = dot(cot_ref[...], w_ref[0]).astype(BF)
        for head in range(HEADS):
            cols = slice(head * HEAD_DIM, (head + 1) * HEAD_DIM)
            scaled = (rows[0, :, cols].astype(F32) * 0.125).astype(BF)
            pair = jnp.concatenate([rows[1, :, cols], rows[2, :, cols]], axis=1)
            for low in range(4):
                kv_ref[position(head, low)] = pair
            qd_ref[head] = jnp.concatenate([scaled, rows[3, :, cols]], axis=1)

    @pl.when(step == 0)
    def _():
        xt_ref[0] = tok_ref[...].T

    @pl.when(step == 1)
    def _():
        xt_ref[1] = cot_ref[...].T


def project(tok, cot, weights):
    rows, width = tok.shape
    whole = lambda step: (0, 0)
    whole3 = lambda step: (0, 0, 0)
    return pl.pallas_call(
        project_kernel,
        grid=(4,),
        in_specs=[
            pl.BlockSpec((rows, width), whole),
            pl.BlockSpec((rows, width), whole),
            pl.BlockSpec((1, width, HEADS * HEAD_DIM), lambda step: (step, 0, 0)),
        ],
        out_specs=[
            pl.BlockSpec((32, rows, 128), whole3),
            pl.BlockSpec((HEADS, rows, 128), whole3),
            pl.BlockSpec((2, width, rows), whole3),
        ],
        out_shape=[
            jax.ShapeDtypeStruct((32, rows, 128), BF),
            jax.ShapeDtypeStruct((HEADS, rows, 128), BF),
            jax.ShapeDtypeStruct((2, width, rows), BF),
        ],
        scratch_shapes=[pltpu.VMEM((4, rows, HEADS * HEAD_DIM), BF)],
        compiler_params=grant(56),
        interpret=INTERPRET,
        name="project",
    )(tok, cot, weights)


def attend_kernel(
    lists_ref, counts_ref, group_ref,
    qd_ref, kvs,
    y_ref, out0, out1, out2, out3,
    kvt, acc, s_scr, p_scr, places,
):
    step = pl.program_id(0)
    group = group_ref[0]
    block = position(step, group)

    @pl.when(step == 0)
    def _():
        for idx in range(32):
            kvt[idx] = kvs[idx].T
        acc[...] = jnp.zeros_like(acc)

    count = counts_ref[block]
    trips = (count + GROUP - 1) // GROUP

    def place(slot):
        raw = lists_ref[block, jnp.minimum(slot, MAXN - 1)]
        where = jnp.where(slot < count, raw, block)
        places[slot] = where
        return where

    qd = qd_ref[0]
    qdt = qd.T
    upper = lax.broadcasted_iota(jnp.int32, (128, 128), 0) < HEAD_DIM
    left = lax.broadcasted_iota(jnp.int32, (128, 128), 1) < HEAD_DIM
    zero = jnp.zeros((128, 128), BF)
    w_in = jnp.concatenate([jnp.where(upper, qdt, zero), jnp.where(upper, zero, qdt)], axis=1)
    w_back = jnp.concatenate([jnp.where(left, qd, zero), jnp.where(left, zero, qd)], axis=0)
    span = GROUP * 128

    def scores(trip, top):
        stack = jnp.concatenate(
            [kvs[place(trip * GROUP + i)] for i in range(GROUP)], axis=0
        )
        both = dot(stack, w_in)
        base = pl.multiple_of(trip * span, span)
        s_scr[pl.ds(base, span), :] = both[:, :128]
        p_scr[pl.ds(base, span), :] = both[:, 128:]
        return jnp.maximum(top, jnp.max(both[:, :128].reshape(span // 8, 8, 128), axis=0))

    top = lax.fori_loop(0, trips, scores, jnp.full((8, 128), -3e38, F32))
    row_max = jnp.max(top, axis=0, keepdims=True)

    def mix(trip, carry):
        total, mixed = carry
        base = pl.multiple_of(trip * span, span)
        parts, values = [], []
        for i in range(GROUP):
            slot = trip * GROUP + i
            shift = jnp.where(slot < count, row_max, 1e30)
            e = jnp.exp(s_scr[pl.ds(base + i * 128, 128), :] - shift)
            s_scr[pl.ds(base + i * 128, 128), :] = e
            total = total + jnp.sum(e.reshape(16, 8, 128), axis=0)
            parts.append(e.astype(BF))
            values.append(kvt[places[slot], HEAD_DIM:, :])
        mixed = mixed + dot(jnp.concatenate(values, axis=1), jnp.concatenate(parts, axis=0))
        return total, mixed

    total, mixed = lax.fori_loop(
        0, trips, mix, (jnp.zeros((8, 128), F32), jnp.zeros((HEAD_DIM, 128), F32))
    )
    inverse = 1.0 / jnp.sum(total, axis=0, keepdims=True)
    attended = (mixed * inverse).astype(BF)
    delta = jnp.sum(
        qdt[HEAD_DIM:, :].astype(F32) * attended.astype(F32), axis=0, keepdims=True
    )

    def back(trip, dq):
        base = pl.multiple_of(trip * span, span)
        dss, pairs, keys, targets = [], [], [], []
        for i in range(GROUP):
            rows = pl.ds(base + i * 128, 128)
            normed = s_scr[rows, :] * inverse
            ds = (normed * (p_scr[rows, :] - delta)).astype(BF)
            dss.append(ds)
            pairs.append(jnp.concatenate([ds, normed.astype(BF)], axis=1))
            where = places[trip * GROUP + i]
            targets.append(where)
            keys.append(kvt[where, :HEAD_DIM, :])
        dq = dq + dot(jnp.concatenate(keys, axis=1), jnp.concatenate(dss, axis=0))
        grads = dot(jnp.concatenate(pairs, axis=0), w_back)
        for i in range(GROUP):
            acc[targets[i]] += grads[i * 128 : (i + 1) * 128]
        return dq

    dq = lax.fori_loop(0, trips, back, jnp.zeros((HEAD_DIM, 128), F32))
    y_ref[0] = jnp.concatenate([dq * 0.125, attended.astype(F32)], axis=0).T.astype(BF)

    @pl.when(step == 7)
    def _():
        for part, ref in enumerate((out0, out1, out2, out3)):
            for idx in range(8):
                ref[idx] = acc[position(idx, group ^ part)].astype(ref.dtype)


def attend(lists, counts, group, qd, kv):
    whole3 = lambda step, *_: (0, 0, 0)
    piece = pl.BlockSpec((8, 128, 128), whole3)
    each = pl.BlockSpec((1, 128, 128), lambda step, *_: (step, 0, 0))
    shape = lambda dtype: jax.ShapeDtypeStruct((8, 128, 128), dtype)
    return pl.pallas_call(
        attend_kernel,
        grid_spec=pltpu.PrefetchScalarGridSpec(
            num_scalar_prefetch=3,
            grid=(8,),
            in_specs=[each, pl.BlockSpec((32, 128, 128), whole3)],
            out_specs=[each] + [piece] * 4,
            scratch_shapes=[
                pltpu.VMEM((32, 128, 128), BF),
                pltpu.VMEM((32, 128, 128), F32),
                pltpu.VMEM((SLOTS * 128, 128), F32),
                pltpu.VMEM((SLOTS * 128, 128), F32),
                pltpu.SMEM((SLOTS,), jnp.int32),
            ],
        ),
        out_shape=[shape(BF), shape(F32), shape(BF), shape(BF), shape(BF)],
        cost_estimate=pl.CostEstimate(
            flops=30_000_000_000, bytes_accessed=4_000_000, transcendentals=4_000_000
        ),
        compiler_params=grant(28),
        interpret=INTERPRET,
        name="attend",
    )(lists, counts, group, qd, kv)


def ordered(y_ref, place):
    return jnp.concatenate([y_ref[place ^ k] for k in (0, 2, 4, 6, 1, 3, 5, 7)], axis=0)


def first_grads_kernel(place_ref, y_ref, *refs):
    xs, out_ref = refs[:8], refs[8]
    y = ordered(y_ref, place_ref[0])
    tok = dot(jnp.concatenate([x[0] for x in xs], axis=1), y)
    cot = dot(jnp.concatenate([x[1] for x in xs], axis=1), y)
    left = lax.broadcasted_iota(jnp.int32, tok.shape, 1) < HEAD_DIM
    out_ref[...] = jnp.where(left, tok, cot)


def second_grads_kernel(place_ref, part0, part1, part2, part3, first_ref, *refs):
    xs, out_ref, mine_refs, y_ref = refs[:8], refs[8], refs[9:17], refs[17]
    y_ref[...] = (
        part0[...]
        + part1[...].astype(F32)
        + part2[...].astype(F32)
        + part3[...].astype(F32)
    ).astype(BF)
    y = ordered(y_ref, place_ref[0])
    for k, ref in enumerate(mine_refs):
        ref[...] = y_ref[place_ref[0] ^ k]
    second = dot(jnp.concatenate([x[0] for x in xs], axis=1), y)
    rows = out_ref.shape[1] // 2
    for index in range(out_ref.shape[0]):
        mine = slice(index * rows, (index + 1) * rows)
        out_ref[index] = jnp.concatenate([first_ref[mine], second[mine]], axis=0).astype(BF)


def grads_call(kernel, place, operands, outs, scratch=()):
    return pl.pallas_call(
        kernel,
        in_specs=[pl.BlockSpec(memory_space=pltpu.SMEM)] + vmem(len(operands)),
        out_specs=vmem(len(outs)),
        out_shape=outs,
        scratch_shapes=list(scratch),
        cost_estimate=pl.CostEstimate(
            flops=2_000_000_000, bytes_accessed=4_000_000, transcendentals=0
        ),
        compiler_params=grant(16),
        interpret=INTERPRET,
    )(place, *operands)


def gather_kernel(in_ref, out_ref):
    replicas, rows = in_ref.shape[0] // 32, in_ref.shape[1] // 2
    parts = []
    for head in range(HEADS):
        total = None
        for low in range(4):
            start = position(head, low) * replicas
            term = jnp.sum(in_ref[start : start + replicas].astype(F32), axis=0)
            total = term if total is None else total + term
        parts.append(total)
    for half, (near, far) in enumerate(((0, 3), (1, 2))):
        mine = slice(half * rows, (half + 1) * rows)
        out_ref[near] = jnp.concatenate([p[mine, :HEAD_DIM] for p in parts], axis=1)
        out_ref[far] = jnp.concatenate([p[mine, HEAD_DIM:] for p in parts], axis=1)


def small_call(kernel, operands, shape, dtype):
    return pl.pallas_call(
        kernel,
        in_specs=vmem(len(operands)),
        out_specs=pl.BlockSpec(memory_space=pltpu.VMEM),
        out_shape=jax.ShapeDtypeStruct(shape, dtype),
        compiler_params=grant(4),
        interpret=INTERPRET,
    )(*operands)


def halves(pieces):
    first = jnp.concatenate([piece[:, :HEAD_DIM] for piece in pieces], axis=1)
    second = jnp.concatenate([piece[:, HEAD_DIM:] for piece in pieces], axis=1)
    return first, second


def output_kernel(y_ref, wq_ref, wo_ref, out_ref, part_ref):
    dq, attended = halves([y_ref[head] for head in range(HEADS)])
    out_ref[...] = dot_t(attended, wo_ref[0]).astype(BF)
    part_ref[...] = dot_t(dq, wq_ref[0])


def inputs_kernel(place_ref, *refs):
    pieces, (part_ref, wk_ref, wv_ref, out_ref, heads) = refs[:8], refs[8:]
    for k, piece in enumerate(pieces):
        heads[place_ref[0] ^ k] = piece[...]
    dk, dv = halves([heads[head] for head in range(HEADS)])
    out_ref[...] = (part_ref[...] + dot_t(dk, wk_ref[0]) + dot_t(dv, wv_ref[0])).astype(BF)


def products_call(kernel, place, arrays, weights, picks, outs, scratch=()):
    whole = lambda array: pl.BlockSpec(array.shape, lambda step: (0,) * array.ndim)
    width = weights.shape[1]
    pick = lambda m: pl.BlockSpec((1, width, HEADS * HEAD_DIM), lambda step: (m, 0, 0))
    return pl.pallas_call(
        kernel,
        grid=(1,),
        in_specs=[pl.BlockSpec(memory_space=pltpu.SMEM) for _ in place]
        + [whole(array) for array in arrays]
        + [pick(m) for m in picks],
        out_specs=[pl.BlockSpec((BLOCK, width), lambda step: (0, 0)) for _ in outs],
        out_shape=[jax.ShapeDtypeStruct((BLOCK, width), dtype) for dtype in outs],
        scratch_shapes=list(scratch),
        cost_estimate=pl.CostEstimate(
            flops=500_000_000, bytes_accessed=4_000_000, transcendentals=0
        ),
        compiler_params=grant(12),
        interpret=INTERPRET,
    )(*place, *arrays, *[weights for _ in picks])


ROW = ("y_low", "x_low")
HEAD = ("y_high", "x_high", "core")
SEQ = ("y_high", "y_low", "x_high", "x_low", "core")


def across(array, axes, flip):
    size = 1 << len(axes)
    return lax.ppermute(array, axes, [(i, i ^ flip) for i in range(size)])


def body(tokens, cotangent, weights, neighbour_lists, neighbour_counts):
    width = tokens.shape[2]
    replicas = lax.axis_size("rep")
    rows = width // (32 * replicas)
    group = lax.axis_index(ROW).astype(jnp.int32).reshape(1)
    place = lax.axis_index(HEAD).astype(jnp.int32).reshape(1)
    swap = lambda array: lax.all_to_all(array, HEAD, 0, 0, tiled=True)

    kv, qd, xt = project(tokens[0], cotangent[0], weights)
    qd = swap(qd)
    kv = lax.all_to_all(kv, SEQ, 0, 0, tiled=True)
    xt, kv = lax.optimization_barrier((xt, kv))
    xs = [xt] + [across(xt, HEAD, k) for k in (2, 4, 6)]
    y, *parts = attend(neighbour_lists[0], neighbour_counts[0], group, qd, kv)
    xs, y = lax.optimization_barrier((xs, y))
    xs = xs + [across(x, HEAD, 1) for x in xs]
    parts = [parts[0]] + [across(parts[k], ROW, k) for k in (1, 2, 3)]
    home = swap(y)
    (first,) = grads_call(
        first_grads_kernel, place, [y, *xs],
        [jax.ShapeDtypeStruct((width, 128), F32)],
    )
    output, partial = products_call(output_kernel, (), (home,), weights, (0, 3), (BF, F32))
    terms, *y2 = grads_call(
        second_grads_kernel, place, [*parts, first, *xs],
        [
            jax.ShapeDtypeStruct((width // rows, 2 * rows, 128), BF),
        ]
        + [jax.ShapeDtypeStruct((128, 128), BF)] * 8,
        [pltpu.VMEM((8, 128, 128), BF)],
    )
    home = y2[:1] + [across(y2[k], HEAD, k) for k in range(1, 8)]
    terms = lax.all_to_all(terms, SEQ + ("rep",), 0, 0, tiled=True)
    (d_inputs,) = products_call(
        inputs_kernel, (place,), (*home, partial), weights, (1, 2), (BF,),
        [pltpu.VMEM((HEADS, BLOCK, 128), BF)],
    )
    summed = small_call(gather_kernel, [terms], (4, rows, HEADS * HEAD_DIM), F32)
    return (output[None], d_inputs[None], summed)


def solution(mesh):
    replicas = mesh.devices.shape[1]
    grid = Mesh(mesh.devices.reshape(2, 2, 2, 2, 2, replicas), SEQ + ("rep",))
    return jax.shard_map(
        body,
        mesh=grid,
        in_specs=(
            P("rep", SEQ, None),
            P("rep", SEQ, None),
            P(),
            P("rep", None, None),
            P("rep", None),
        ),
        out_specs=(
            P("rep", SEQ, None),
            P("rep", SEQ, None),
            P(None, SEQ + ("rep",), None),
        ),
        check_vma=False,
    )
```

```python
import jax
import jax.numpy as jnp
from jax import lax
from jax.experimental import pallas as pl
from jax.experimental.pallas import tpu as pltpu
from jax.sharding import Mesh, PartitionSpec as P


HEADS = 8
HEAD_DIM = 64
BLOCK = 128
MAXN = 27
GROUP = 4
SLOTS = 28
BF = jnp.bfloat16
F32 = jnp.float32
INTERPRET = False


def dot(a, b):
    return jnp.dot(a, b, preferred_element_type=F32)


def dot_t(a, b):
    return lax.dot_general(a, b, (((1,), (1,)), ((), ())), preferred_element_type=F32)


def grant(mib):
    return pltpu.CompilerParams(vmem_limit_bytes=mib << 20)


def vmem(count):
    return [pl.BlockSpec(memory_space=pltpu.VMEM) for _ in range(count)]


def hbm(count):
    return [pl.BlockSpec(memory_space=pltpu.HBM) for _ in range(count)]


def position(high, low):
    return low * 8 + high


def project_kernel(tok_ref, cot_ref, w_ref, kv_ref, qd_ref, xt_ref, rows):
    step = pl.program_id(0)

    @pl.when(step < 3)
    def _():
        rows[step] = dot(tok_ref[...], w_ref[0]).astype(BF)

    @pl.when(step == 3)
    def _():
        rows[3] = dot(cot_ref[...], w_ref[0]).astype(BF)
        for head in range(HEADS):
            cols = slice(head * HEAD_DIM, (head + 1) * HEAD_DIM)
            scaled = (rows[0, :, cols].astype(F32) * 0.125).astype(BF)
            kv_ref[head] = jnp.concatenate([rows[1, :, cols], rows[2, :, cols]], axis=1)
            qd_ref[head] = jnp.concatenate([scaled, rows[3, :, cols]], axis=1)

    @pl.when(step == 0)
    def _():
        xt_ref[0] = tok_ref[...].T

    @pl.when(step == 1)
    def _():
        xt_ref[1] = cot_ref[...].T


def project(tok, cot, weights):
    rows, width = tok.shape
    whole = lambda step: (0, 0)
    whole3 = lambda step: (0, 0, 0)
    return pl.pallas_call(
        project_kernel,
        grid=(4,),
        in_specs=[
            pl.BlockSpec((rows, width), whole),
            pl.BlockSpec((rows, width), whole),
            pl.BlockSpec((1, width, HEADS * HEAD_DIM), lambda step: (step, 0, 0)),
        ],
        out_specs=[
            pl.BlockSpec((HEADS, rows, 128), whole3),
            pl.BlockSpec((HEADS, rows, 128), whole3),
            pl.BlockSpec((2, width, rows), whole3),
        ],
        out_shape=[
            jax.ShapeDtypeStruct((HEADS, rows, 128), BF),
            jax.ShapeDtypeStruct((HEADS, rows, 128), BF),
            jax.ShapeDtypeStruct((2, width, rows), BF),
        ],
        scratch_shapes=[pltpu.VMEM((4, rows, HEADS * HEAD_DIM), BF)],
        compiler_params=grant(56),
        interpret=INTERPRET,
        name="project",
    )(tok, cot, weights)


def attend_kernel(
    lists_ref, counts_ref, group_ref,
    qd_ref, kv0, kv1, kv2, kv3,
    y_ref, out0, out1, out2, out3,
    kvs, kvt, acc, s_scr, p_scr, places, sems,
):
    step = pl.program_id(0)
    group = group_ref[0]
    block = position(step, group)

    @pl.when(step == 0)
    def _():
        copies = [
            pltpu.make_async_copy(ref, kvs.at[pl.ds(8 * part, 8)], sems.at[part])
            for part, ref in enumerate((kv0, kv1, kv2, kv3))
        ]
        for copy in copies:
            copy.start()
        acc[...] = jnp.zeros_like(acc)
        for part, copy in enumerate(copies):
            copy.wait()
            for idx in range(8 * part, 8 * part + 8):
                kvt[idx] = kvs[idx].T

    count = counts_ref[block]
    trips = (count + GROUP - 1) // GROUP

    def place(slot):
        raw = lists_ref[block, jnp.minimum(slot, MAXN - 1)]
        raw = jnp.where(slot < count, raw, block)
        where = raw ^ (group * 8)
        places[slot] = where
        return where

    qd = qd_ref[0]
    qdt = qd.T
    upper = lax.broadcasted_iota(jnp.int32, (128, 128), 0) < HEAD_DIM
    left = lax.broadcasted_iota(jnp.int32, (128, 128), 1) < HEAD_DIM
    zero = jnp.zeros((128, 128), BF)
    w_in = jnp.concatenate([jnp.where(upper, qdt, zero), jnp.where(upper, zero, qdt)], axis=1)
    w_back = jnp.concatenate([jnp.where(left, qd, zero), jnp.where(left, zero, qd)], axis=0)
    span = GROUP * 128

    def scores(trip, top):
        stack = jnp.concatenate(
            [kvs[place(trip * GROUP + i)] for i in range(GROUP)], axis=0
        )
        both = dot(stack, w_in)
        base = pl.multiple_of(trip * span, span)
        s_scr[pl.ds(base, span), :] = both[:, :128]
        p_scr[pl.ds(base, span), :] = both[:, 128:]
        return jnp.maximum(top, jnp.max(both[:, :128].reshape(span // 8, 8, 128), axis=0))

    top = lax.fori_loop(0, trips, scores, jnp.full((8, 128), -3e38, F32))
    row_max = jnp.max(top, axis=0, keepdims=True)

    def mix(trip, carry):
        total, mixed = carry
        base = pl.multiple_of(trip * span, span)
        parts, values = [], []
        for i in range(GROUP):
            slot = trip * GROUP + i
            shift = jnp.where(slot < count, row_max, 1e30)
            e = jnp.exp(s_scr[pl.ds(base + i * 128, 128), :] - shift)
            s_scr[pl.ds(base + i * 128, 128), :] = e
            total = total + jnp.sum(e.reshape(16, 8, 128), axis=0)
            parts.append(e.astype(BF))
            values.append(kvt[places[slot], HEAD_DIM:, :])
        mixed = mixed + dot(jnp.concatenate(values, axis=1), jnp.concatenate(parts, axis=0))
        return total, mixed

    total, mixed = lax.fori_loop(
        0, trips, mix, (jnp.zeros((8, 128), F32), jnp.zeros((HEAD_DIM, 128), F32))
    )
    inverse = 1.0 / jnp.sum(total, axis=0, keepdims=True)
    attended = (mixed * inverse).astype(BF)
    delta = jnp.sum(
        qdt[HEAD_DIM:, :].astype(F32) * attended.astype(F32), axis=0, keepdims=True
    )

    def back(trip, dq):
        base = pl.multiple_of(trip * span, span)
        dss, pairs, keys, targets = [], [], [], []
        for i in range(GROUP):
            rows = pl.ds(base + i * 128, 128)
            normed = s_scr[rows, :] * inverse
            ds = (normed * (p_scr[rows, :] - delta)).astype(BF)
            dss.append(ds)
            pairs.append(jnp.concatenate([ds, normed.astype(BF)], axis=1))
            where = places[trip * GROUP + i]
            targets.append(where)
            keys.append(kvt[where, :HEAD_DIM, :])
        dq = dq + dot(jnp.concatenate(keys, axis=1), jnp.concatenate(dss, axis=0))
        grads = dot(jnp.concatenate(pairs, axis=0), w_back)
        for i in range(GROUP):
            acc[targets[i]] += grads[i * 128 : (i + 1) * 128]
        return dq

    dq = lax.fori_loop(0, trips, back, jnp.zeros((HEAD_DIM, 128), F32))
    y_ref[0] = jnp.concatenate([dq * 0.125, attended.astype(F32)], axis=0).T.astype(BF)

    @pl.when(step == 7)
    def _():
        for part, ref in enumerate((out0, out1, out2, out3)):
            for idx in range(8):
                ref[idx] = acc[8 * part + idx].astype(ref.dtype)


def attend(lists, counts, group, qd, kvs):
    whole3 = lambda step, *_: (0, 0, 0)
    piece = pl.BlockSpec((8, 128, 128), whole3)
    each = pl.BlockSpec((1, 128, 128), lambda step, *_: (step, 0, 0))
    shape = lambda dtype: jax.ShapeDtypeStruct((8, 128, 128), dtype)
    return pl.pallas_call(
        attend_kernel,
        grid_spec=pltpu.PrefetchScalarGridSpec(
            num_scalar_prefetch=3,
            grid=(8,),
            in_specs=[each] + hbm(4),
            out_specs=[each] + [piece] * 4,
            scratch_shapes=[
                pltpu.VMEM((32, 128, 128), BF),
                pltpu.VMEM((32, 128, 128), BF),
                pltpu.VMEM((32, 128, 128), F32),
                pltpu.VMEM((SLOTS * 128, 128), F32),
                pltpu.VMEM((SLOTS * 128, 128), F32),
                pltpu.SMEM((SLOTS,), jnp.int32),
                pltpu.SemaphoreType.DMA((4,)),
            ],
        ),
        out_shape=[shape(BF), shape(F32), shape(BF), shape(BF), shape(BF)],
        cost_estimate=pl.CostEstimate(
            flops=30_000_000_000, bytes_accessed=4_000_000, transcendentals=4_000_000
        ),
        compiler_params=grant(28),
        interpret=INTERPRET,
        name="attend",
    )(lists, counts, group, qd, *kvs)


def ordered(y_ref, place):
    return jnp.concatenate([y_ref[place ^ k] for k in (0, 2, 4, 6, 1, 3, 5, 7)], axis=0)


def first_grads_kernel(place_ref, y_ref, *refs):
    xs, out_ref = refs[:8], refs[8]
    y = ordered(y_ref, place_ref[0])
    tok = dot(jnp.concatenate([x[0] for x in xs], axis=1), y)
    cot = dot(jnp.concatenate([x[1] for x in xs], axis=1), y)
    left = lax.broadcasted_iota(jnp.int32, tok.shape, 1) < HEAD_DIM
    out_ref[...] = jnp.where(left, tok, cot)


def second_grads_kernel(place_ref, own, part1, part2, part3, first_ref, *refs):
    xs, (out_ref, keep_ref, send_ref, y_ref, base, landed, sems) = refs[:8], refs[8:]
    copies = [pltpu.make_async_copy(own, base, sems.at[0])] + [
        pltpu.make_async_copy(part, landed.at[k], sems.at[k + 1])
        for k, part in enumerate((part1, part2, part3))
    ]
    for copy in copies:
        copy.start()
    for copy in copies:
        copy.wait()
    y_ref[...] = (base[...] + jnp.sum(landed[...].astype(F32), axis=0)).astype(BF)
    chip, core = place_ref[0] // 2, lax.rem(place_ref[0], 2)
    for k in range(4):
        keep_ref[k] = y_ref[(chip ^ k) * 2 + core]
        send_ref[k] = y_ref[(chip ^ k) * 2 + 1 - core]
    y = ordered(y_ref, place_ref[0])
    second = dot(jnp.concatenate([x[0] for x in xs], axis=1), y)
    rows = out_ref.shape[1] // 2
    for index in range(out_ref.shape[0]):
        mine = slice(index * rows, (index + 1) * rows)
        out_ref[index] = jnp.concatenate([first_ref[mine], second[mine]], axis=0).astype(BF)


def pack_kernel(keep_ref, got_ref, *outs):
    for k, ref in enumerate(outs):
        ref[0] = keep_ref[k + 1]
        ref[1] = got_ref[k + 1]


def grads_call(kernel, place, specs, operands, outs, scratch=()):
    return pl.pallas_call(
        kernel,
        in_specs=[pl.BlockSpec(memory_space=pltpu.SMEM)] + specs,
        out_specs=vmem(len(outs)),
        out_shape=outs,
        scratch_shapes=list(scratch),
        cost_estimate=pl.CostEstimate(
            flops=2_000_000_000, bytes_accessed=4_000_000, transcendentals=0
        ),
        compiler_params=grant(16),
        interpret=INTERPRET,
    )(place, *operands)


def gather_kernel(in_ref, out_ref):
    replicas, rows = in_ref.shape[0] // 32, in_ref.shape[1] // 2
    parts = []
    for head in range(HEADS):
        total = None
        for low in range(4):
            start = position(head, low) * replicas
            term = jnp.sum(in_ref[start : start + replicas].astype(F32), axis=0)
            total = term if total is None else total + term
        parts.append(total)
    for half, (near, far) in enumerate(((0, 3), (1, 2))):
        mine = slice(half * rows, (half + 1) * rows)
        out_ref[near] = jnp.concatenate([p[mine, :HEAD_DIM] for p in parts], axis=1)
        out_ref[far] = jnp.concatenate([p[mine, HEAD_DIM:] for p in parts], axis=1)


def small_call(kernel, operands, outs):
    return pl.pallas_call(
        kernel,
        in_specs=vmem(len(operands)),
        out_specs=vmem(len(outs)),
        out_shape=outs,
        compiler_params=grant(4),
        interpret=INTERPRET,
    )(*operands)


def halves(pieces):
    first = jnp.concatenate([piece[:, :HEAD_DIM] for piece in pieces], axis=1)
    second = jnp.concatenate([piece[:, HEAD_DIM:] for piece in pieces], axis=1)
    return first, second


def output_kernel(y_ref, wq_ref, wo_ref, out_ref, part_ref):
    dq, attended = halves([y_ref[head] for head in range(HEADS)])
    out_ref[...] = dot_t(attended, wo_ref[0]).astype(BF)
    part_ref[...] = dot_t(dq, wq_ref[0])


def inputs_kernel(place_ref, keep_ref, got_ref, *refs):
    pairs, (part_ref, wk_ref, wv_ref, out_ref, heads) = refs[:3], refs[3:]
    place = place_ref[0]
    heads[place] = keep_ref[0]
    heads[place ^ 1] = got_ref[0]
    for k, pair in enumerate(pairs):
        heads[place ^ (2 * k + 2)] = pair[0]
        heads[place ^ (2 * k + 3)] = pair[1]
    dk, dv = halves([heads[head] for head in range(HEADS)])
    out_ref[...] = (part_ref[...] + dot_t(dk, wk_ref[0]) + dot_t(dv, wv_ref[0])).astype(BF)


def products_call(kernel, place, arrays, weights, picks, outs, scratch=()):
    whole = lambda array: pl.BlockSpec(array.shape, lambda step: (0,) * array.ndim)
    width = weights.shape[1]
    pick = lambda m: pl.BlockSpec((1, width, HEADS * HEAD_DIM), lambda step: (m, 0, 0))
    return pl.pallas_call(
        kernel,
        grid=(1,),
        in_specs=[pl.BlockSpec(memory_space=pltpu.SMEM) for _ in place]
        + [whole(array) for array in arrays]
        + [pick(m) for m in picks],
        out_specs=[pl.BlockSpec((BLOCK, width), lambda step: (0, 0)) for _ in outs],
        out_shape=[jax.ShapeDtypeStruct((BLOCK, width), dtype) for dtype in outs],
        scratch_shapes=list(scratch),
        cost_estimate=pl.CostEstimate(
            flops=500_000_000, bytes_accessed=4_000_000, transcendentals=0
        ),
        compiler_params=grant(12),
        interpret=INTERPRET,
    )(*place, *arrays, *[weights for _ in picks])


ROW = ("row",)
HEAD = ("head",)
SEQ = ROW + HEAD


def across(array, axes, flip):
    return lax.ppermute(array, axes, [(i, i ^ flip) for i in range(lax.axis_size(axes))])


def body(tokens, cotangent, weights, neighbour_lists, neighbour_counts):
    width = tokens.shape[2]
    rows = width // (32 * lax.axis_size("rep"))
    group = lax.axis_index(ROW).astype(jnp.int32).reshape(1)
    place = lax.axis_index(HEAD).astype(jnp.int32).reshape(1)
    swap = lambda array: lax.all_to_all(array, HEAD, 0, 0, tiled=True)
    kv, qd, xt = project(tokens[0], cotangent[0], weights)
    kv = swap(kv)
    qd, xt, kv = lax.optimization_barrier((qd, xt, kv))
    kvs = [kv] + [across(kv, ROW, k) for k in (1, 2, 3)]
    qd = swap(qd)
    xs = [xt] + [across(xt, HEAD, k) for k in (2, 4, 6)]
    y, *parts = attend(neighbour_lists[0], neighbour_counts[0], group, qd, kvs)
    xs, y = lax.optimization_barrier((xs, y))
    xs = xs + [across(x, HEAD, 1) for x in xs]
    parts = [parts[0]] + [across(parts[k], ROW, k) for k in (1, 2, 3)]
    home = swap(y)
    (first,) = grads_call(
        first_grads_kernel, place, vmem(9), [y, *xs],
        [jax.ShapeDtypeStruct((width, 128), F32)],
    )
    output, partial = products_call(output_kernel, (), (home,), weights, (0, 3), (BF, F32))
    pieces = lambda count: jax.ShapeDtypeStruct((count, 128, 128), BF)
    terms, keep, send = grads_call(
        second_grads_kernel, place, hbm(4) + vmem(9),
        [*parts, first, *xs],
        [jax.ShapeDtypeStruct((width // rows, 2 * rows, 128), BF), pieces(4), pieces(4)],
        [
            pltpu.VMEM((8, 128, 128), BF),
            pltpu.VMEM((8, 128, 128), F32),
            pltpu.VMEM((3, 8, 128, 128), BF),
            pltpu.SemaphoreType.DMA((4,)),
        ],
    )
    terms = lax.all_to_all(terms, SEQ + ("rep",), 0, 0, tiled=True)
    got = across(send, HEAD, 1)
    pairs = small_call(pack_kernel, [keep, got], [pieces(2)] * 3)
    pairs = [across(pair, HEAD, 2 * k + 2) for k, pair in enumerate(pairs)]
    (d_inputs,) = products_call(
        inputs_kernel, (place,), (keep, got, *pairs, partial), weights, (1, 2),
        (BF,), [pltpu.VMEM((HEADS, BLOCK, 128), BF)],
    )
    (summed,) = small_call(
        gather_kernel, [terms],
        [jax.ShapeDtypeStruct((4, rows, HEADS * HEAD_DIM), F32)],
    )
    return (output[None], d_inputs[None], summed)


def solution(mesh):
    replicas = mesh.devices.shape[1]
    grid = Mesh(mesh.devices.reshape(4, 8, replicas), SEQ + ("rep",))
    return jax.shard_map(
        body,
        mesh=grid,
        in_specs=(
            P("rep", SEQ, None),
            P("rep", SEQ, None),
            P(),
            P("rep", None, None),
            P("rep", None),
        ),
        out_specs=(
            P("rep", SEQ, None),
            P("rep", SEQ, None),
            P(None, SEQ + ("rep",), None),
        ),
        check_vma=False,
    )
```

```python
import jax
import jax.numpy as jnp
from jax import lax
from jax.experimental import pallas as pl
from jax.experimental.pallas import tpu as pltpu
from jax.sharding import Mesh, PartitionSpec as P


HEADS = 8
HEAD_DIM = 64
BLOCK = 128
MAXN = 27
LARGE, SMALL = 8, 4
SLOTS = 28
BF = jnp.bfloat16
F32 = jnp.float32
INTERPRET = False


def dot(a, b):
    return jnp.dot(a, b, preferred_element_type=F32)


def dot_t(a, b):
    return lax.dot_general(a, b, (((1,), (1,)), ((), ())), preferred_element_type=F32)


def grant(mib):
    return pltpu.CompilerParams(vmem_limit_bytes=mib << 20)


def vmem(count):
    return [pl.BlockSpec(memory_space=pltpu.VMEM) for _ in range(count)]


def hbm(count):
    return [pl.BlockSpec(memory_space=pltpu.HBM) for _ in range(count)]


def position(high, low):
    return low * 8 + high


def project_kernel(tok_ref, cot_ref, w_ref, kv_ref, qd_ref, xt_ref, rows):
    step = pl.program_id(0)

    @pl.when(step < 3)
    def _():
        rows[step] = dot(tok_ref[...], w_ref[0]).astype(BF)

    @pl.when(step == 3)
    def _():
        rows[3] = dot(cot_ref[...], w_ref[0]).astype(BF)
        for head in range(HEADS):
            cols = slice(head * HEAD_DIM, (head + 1) * HEAD_DIM)
            scaled = (rows[0, :, cols].astype(F32) * 0.125).astype(BF)
            kv_ref[head] = jnp.concatenate([rows[1, :, cols], rows[2, :, cols]], axis=1)
            qd_ref[head] = jnp.concatenate([scaled, rows[3, :, cols]], axis=1)

    @pl.when(step == 0)
    def _():
        xt_ref[0] = tok_ref[...].T

    @pl.when(step == 1)
    def _():
        xt_ref[1] = cot_ref[...].T


def project(tok, cot, weights):
    rows, width = tok.shape
    whole = lambda step: (0, 0)
    whole3 = lambda step: (0, 0, 0)
    return pl.pallas_call(
        project_kernel,
        grid=(4,),
        in_specs=[
            pl.BlockSpec((rows, width), whole),
            pl.BlockSpec((rows, width), whole),
            pl.BlockSpec((1, width, HEADS * HEAD_DIM), lambda step: (step, 0, 0)),
        ],
        out_specs=[
            pl.BlockSpec((HEADS, rows, 128), whole3),
            pl.BlockSpec((HEADS, rows, 128), whole3),
            pl.BlockSpec((2, width, rows), whole3),
        ],
        out_shape=[
            jax.ShapeDtypeStruct((HEADS, rows, 128), BF),
            jax.ShapeDtypeStruct((HEADS, rows, 128), BF),
            jax.ShapeDtypeStruct((2, width, rows), BF),
        ],
        scratch_shapes=[pltpu.VMEM((4, rows, HEADS * HEAD_DIM), BF)],
        compiler_params=grant(56),
        interpret=INTERPRET,
        name="project",
    )(tok, cot, weights)


def attend_kernel(
    lists_ref, counts_ref, group_ref,
    qd_ref, kv0, kv1, kv2, kv3,
    y_ref, out0, out1, out2, out3,
    kvs, kvt, acc, s_scr, p_scr, ds_scr, n_scr, w_in, w_back, places, sems,
):
    step = pl.program_id(0)
    group = group_ref[0]
    block = position(step, group)

    @pl.when(step == 0)
    def _():
        copies = [
            pltpu.make_async_copy(ref, kvs.at[pl.ds(8 * part, 8)], sems.at[part])
            for part, ref in enumerate((kv0, kv1, kv2, kv3))
        ]
        for copy in copies:
            copy.start()
        acc[...] = jnp.zeros_like(acc)
        for part, copy in enumerate(copies):
            copy.wait()
            for idx in range(8 * part, 8 * part + 8):
                kvt[idx] = kvs[idx].T

    count = counts_ref[block]
    large = (count + SMALL - 1) // LARGE
    small = (count - large * LARGE + SMALL - 1) // SMALL

    def sweep(visit, carry):
        carry = lax.fori_loop(0, large, lambda i, c: visit(LARGE, i * LARGE, c), carry)
        return lax.fori_loop(
            0, small, lambda i, c: visit(SMALL, large * LARGE + i * SMALL, c), carry
        )

    def place(slot):
        raw = lists_ref[block, jnp.minimum(slot, MAXN - 1)]
        raw = jnp.where(slot < count, raw, block)
        where = raw ^ (group * 8)
        places[slot] = where
        return where

    qd = qd_ref[0]
    qdt = qd.T
    upper = lax.broadcasted_iota(jnp.int32, (128, 128), 0) < HEAD_DIM
    left = lax.broadcasted_iota(jnp.int32, (128, 128), 1) < HEAD_DIM
    zero = jnp.zeros((128, 128), BF)
    w_in[:, :128] = jnp.where(upper, qdt, zero)
    w_in[:, 128:] = jnp.where(upper, zero, qdt)
    w_back[:128] = jnp.where(left, qd, zero)
    w_back[128:] = jnp.where(left, zero, qd)

    def rows_of(slot, size):
        return pl.ds(pl.multiple_of(slot * 128, 128), size * 128)

    def scores(size, slot, top):
        stack = jnp.concatenate([kvs[place(slot + i)] for i in range(size)], axis=0)
        both = dot(stack, w_in[...])
        s_scr[rows_of(slot, size), :] = both[:, :128]
        p_scr[rows_of(slot, size), :] = both[:, 128:]
        return jnp.maximum(top, jnp.max(both[:, :128].reshape(size * 16, 8, 128), axis=0))

    top = sweep(scores, jnp.full((8, 128), -3e38, F32))
    row_max = jnp.max(top, axis=0, keepdims=True)

    def mix(size, slot, carry):
        total, mixed = carry
        parts, values = [], []
        for i in range(size):
            shift = jnp.where(slot + i < count, row_max, 1e30)
            e = jnp.exp(s_scr[rows_of(slot + i, 1), :] - shift)
            s_scr[rows_of(slot + i, 1), :] = e
            total = total + jnp.sum(e.reshape(16, 8, 128), axis=0)
            parts.append(e.astype(BF))
            values.append(kvt[places[slot + i], HEAD_DIM:, :])
        mixed = mixed + dot(jnp.concatenate(values, axis=1), jnp.concatenate(parts, axis=0))
        return total, mixed

    total, mixed = sweep(mix, (jnp.zeros((8, 128), F32), jnp.zeros((HEAD_DIM, 128), F32)))
    inverse = 1.0 / jnp.sum(total, axis=0, keepdims=True)
    attended = (mixed * inverse).astype(BF)
    delta = jnp.sum(
        qdt[HEAD_DIM:, :].astype(F32) * attended.astype(F32), axis=0, keepdims=True
    )

    def back(size, slot, dq):
        keys = []
        for i in range(size):
            rows, here = rows_of(slot + i, 1), slice(i * 128, (i + 1) * 128)
            normed = s_scr[rows, :] * inverse
            ds_scr[here, :] = (normed * (p_scr[rows, :] - delta)).astype(BF)
            n_scr[here, :] = normed.astype(BF)
            keys.append(kvt[places[slot + i], :HEAD_DIM, :])
        span = slice(0, size * 128)
        dq = dq + dot(jnp.concatenate(keys, axis=1), ds_scr[span, :])
        grads = dot(jnp.concatenate([ds_scr[span, :], n_scr[span, :]], axis=1), w_back[...])
        for i in range(size):
            acc[places[slot + i]] += grads[i * 128 : (i + 1) * 128]
        return dq

    dq = sweep(back, jnp.zeros((HEAD_DIM, 128), F32))
    y_ref[0] = jnp.concatenate([dq * 0.125, attended.astype(F32)], axis=0).T.astype(BF)

    @pl.when(step == 7)
    def _():
        for part, ref in enumerate((out0, out1, out2, out3)):
            for idx in range(8):
                ref[idx] = acc[8 * part + idx].astype(ref.dtype)


def attend(lists, counts, group, qd, kvs):
    whole3 = lambda step, *_: (0, 0, 0)
    piece = pl.BlockSpec((8, 128, 128), whole3)
    each = pl.BlockSpec((1, 128, 128), lambda step, *_: (step, 0, 0))
    shape = lambda dtype: jax.ShapeDtypeStruct((8, 128, 128), dtype)
    return pl.pallas_call(
        attend_kernel,
        grid_spec=pltpu.PrefetchScalarGridSpec(
            num_scalar_prefetch=3,
            grid=(8,),
            in_specs=[each] + hbm(4),
            out_specs=[each] + [piece] * 4,
            scratch_shapes=[
                pltpu.VMEM((32, 128, 128), BF),
                pltpu.VMEM((32, 128, 128), BF),
                pltpu.VMEM((32, 128, 128), F32),
                pltpu.VMEM((SLOTS * 128, 128), F32),
                pltpu.VMEM((SLOTS * 128, 128), F32),
                pltpu.VMEM((LARGE * 128, 128), BF),
                pltpu.VMEM((LARGE * 128, 128), BF),
                pltpu.VMEM((128, 256), BF),
                pltpu.VMEM((256, 128), BF),
                pltpu.SMEM((SLOTS,), jnp.int32),
                pltpu.SemaphoreType.DMA((4,)),
            ],
        ),
        out_shape=[shape(BF), shape(F32), shape(BF), shape(BF), shape(BF)],
        cost_estimate=pl.CostEstimate(
            flops=30_000_000_000, bytes_accessed=4_000_000, transcendentals=4_000_000
        ),
        compiler_params=grant(28),
        interpret=INTERPRET,
        name="attend",
    )(lists, counts, group, qd, *kvs)


def ordered(y_ref, place):
    return jnp.concatenate([y_ref[place ^ k] for k in (0, 2, 4, 6, 1, 3, 5, 7)], axis=0)


def first_grads_kernel(place_ref, y_ref, *refs):
    xs, out_ref = refs[:8], refs[8]
    y = ordered(y_ref, place_ref[0])
    tok = dot(jnp.concatenate([x[0] for x in xs], axis=1), y)
    cot = dot(jnp.concatenate([x[1] for x in xs], axis=1), y)
    left = lax.broadcasted_iota(jnp.int32, tok.shape, 1) < HEAD_DIM
    out_ref[...] = jnp.where(left, tok, cot)


def second_grads_kernel(place_ref, own, part1, part2, part3, first_ref, *refs):
    xs, (out_ref, keep_ref, send_ref, y_ref, base, landed, sems) = refs[:8], refs[8:]
    copies = [pltpu.make_async_copy(own, base, sems.at[0])] + [
        pltpu.make_async_copy(part, landed.at[k], sems.at[k + 1])
        for k, part in enumerate((part1, part2, part3))
    ]
    for copy in copies:
        copy.start()
    for copy in copies:
        copy.wait()
    y_ref[...] = (base[...] + jnp.sum(landed[...].astype(F32), axis=0)).astype(BF)
    chip, core = place_ref[0] // 2, lax.rem(place_ref[0], 2)
    for k in range(4):
        keep_ref[k] = y_ref[(chip ^ k) * 2 + core]
        send_ref[k] = y_ref[(chip ^ k) * 2 + 1 - core]
    y = ordered(y_ref, place_ref[0])
    second = dot(jnp.concatenate([x[0] for x in xs], axis=1), y)
    rows = out_ref.shape[1] // 2
    for index in range(out_ref.shape[0]):
        mine = slice(index * rows, (index + 1) * rows)
        out_ref[index] = jnp.concatenate([first_ref[mine], second[mine]], axis=0).astype(BF)


def pack_kernel(keep_ref, got_ref, *outs):
    for k, ref in enumerate(outs):
        ref[0] = keep_ref[k + 1]
        ref[1] = got_ref[k + 1]


def grads_call(kernel, place, specs, operands, outs, scratch=()):
    return pl.pallas_call(
        kernel,
        in_specs=[pl.BlockSpec(memory_space=pltpu.SMEM)] + specs,
        out_specs=vmem(len(outs)),
        out_shape=outs,
        scratch_shapes=list(scratch),
        cost_estimate=pl.CostEstimate(
            flops=2_000_000_000, bytes_accessed=4_000_000, transcendentals=0
        ),
        compiler_params=grant(16),
        interpret=INTERPRET,
    )(place, *operands)


def gather_kernel(in_ref, out_ref):
    replicas, rows = in_ref.shape[0] // 32, in_ref.shape[1] // 2
    parts = []
    for head in range(HEADS):
        total = None
        for low in range(4):
            start = position(head, low) * replicas
            term = jnp.sum(in_ref[start : start + replicas].astype(F32), axis=0)
            total = term if total is None else total + term
        parts.append(total)
    for half, (near, far) in enumerate(((0, 3), (1, 2))):
        mine = slice(half * rows, (half + 1) * rows)
        out_ref[near] = jnp.concatenate([p[mine, :HEAD_DIM] for p in parts], axis=1)
        out_ref[far] = jnp.concatenate([p[mine, HEAD_DIM:] for p in parts], axis=1)


def small_call(kernel, operands, outs):
    return pl.pallas_call(
        kernel,
        in_specs=vmem(len(operands)),
        out_specs=vmem(len(outs)),
        out_shape=outs,
        compiler_params=grant(4),
        interpret=INTERPRET,
    )(*operands)


def halves(pieces):
    first = jnp.concatenate([piece[:, :HEAD_DIM] for piece in pieces], axis=1)
    second = jnp.concatenate([piece[:, HEAD_DIM:] for piece in pieces], axis=1)
    return first, second


def output_kernel(y_ref, wq_ref, wo_ref, out_ref, part_ref):
    dq, attended = halves([y_ref[head] for head in range(HEADS)])
    out_ref[...] = dot_t(attended, wo_ref[0]).astype(BF)
    part_ref[...] = dot_t(dq, wq_ref[0])


def inputs_kernel(place_ref, keep_ref, got_ref, *refs):
    pairs, (part_ref, wk_ref, wv_ref, out_ref, heads) = refs[:3], refs[3:]
    place = place_ref[0]
    heads[place] = keep_ref[0]
    heads[place ^ 1] = got_ref[0]
    for k, pair in enumerate(pairs):
        heads[place ^ (2 * k + 2)] = pair[0]
        heads[place ^ (2 * k + 3)] = pair[1]
    dk, dv = halves([heads[head] for head in range(HEADS)])
    out_ref[...] = (part_ref[...] + dot_t(dk, wk_ref[0]) + dot_t(dv, wv_ref[0])).astype(BF)


def products_call(kernel, place, arrays, weights, picks, outs, scratch=()):
    whole = lambda array: pl.BlockSpec(array.shape, lambda step: (0,) * array.ndim)
    width = weights.shape[1]
    pick = lambda m: pl.BlockSpec((1, width, HEADS * HEAD_DIM), lambda step: (m, 0, 0))
    return pl.pallas_call(
        kernel,
        grid=(1,),
        in_specs=[pl.BlockSpec(memory_space=pltpu.SMEM) for _ in place]
        + [whole(array) for array in arrays]
        + [pick(m) for m in picks],
        out_specs=[pl.BlockSpec((BLOCK, width), lambda step: (0, 0)) for _ in outs],
        out_shape=[jax.ShapeDtypeStruct((BLOCK, width), dtype) for dtype in outs],
        scratch_shapes=list(scratch),
        cost_estimate=pl.CostEstimate(
            flops=500_000_000, bytes_accessed=4_000_000, transcendentals=0
        ),
        compiler_params=grant(12),
        interpret=INTERPRET,
    )(*place, *arrays, *[weights for _ in picks])


ROW = ("row",)
HEAD = ("head",)
SEQ = ROW + HEAD


def across(array, axes, flip):
    return lax.ppermute(array, axes, [(i, i ^ flip) for i in range(lax.axis_size(axes))])


def body(tokens, cotangent, weights, neighbour_lists, neighbour_counts):
    width = tokens.shape[2]
    rows = width // (32 * lax.axis_size("rep"))
    group = lax.axis_index(ROW).astype(jnp.int32).reshape(1)
    place = lax.axis_index(HEAD).astype(jnp.int32).reshape(1)
    swap = lambda array: lax.all_to_all(array, HEAD, 0, 0, tiled=True)
    kv, qd, xt = project(tokens[0], cotangent[0], weights)
    kv = swap(kv)
    qd, xt, kv = lax.optimization_barrier((qd, xt, kv))
    kvs = [kv] + [across(kv, ROW, k) for k in (1, 2, 3)]
    qd = swap(qd)
    xs = [xt] + [across(xt, HEAD, k) for k in (2, 4, 6)]
    y, *parts = attend(neighbour_lists[0], neighbour_counts[0], group, qd, kvs)
    xs, y = lax.optimization_barrier((xs, y))
    xs = xs + [across(x, HEAD, 1) for x in xs]
    parts = [parts[0]] + [across(parts[k], ROW, k) for k in (1, 2, 3)]
    home = swap(y)
    (first,) = grads_call(
        first_grads_kernel, place, vmem(9), [y, *xs],
        [jax.ShapeDtypeStruct((width, 128), F32)],
    )
    output, partial = products_call(output_kernel, (), (home,), weights, (0, 3), (BF, F32))
    pieces = lambda count: jax.ShapeDtypeStruct((count, 128, 128), BF)
    terms, keep, send = grads_call(
        second_grads_kernel, place, hbm(4) + vmem(9),
        [*parts, first, *xs],
        [jax.ShapeDtypeStruct((width // rows, 2 * rows, 128), BF), pieces(4), pieces(4)],
        [
            pltpu.VMEM((8, 128, 128), BF),
            pltpu.VMEM((8, 128, 128), F32),
            pltpu.VMEM((3, 8, 128, 128), BF),
            pltpu.SemaphoreType.DMA((4,)),
        ],
    )
    terms = lax.all_to_all(terms, SEQ + ("rep",), 0, 0, tiled=True)
    got = across(send, HEAD, 1)
    pairs = small_call(pack_kernel, [keep, got], [pieces(2)] * 3)
    pairs = [across(pair, HEAD, 2 * k + 2) for k, pair in enumerate(pairs)]
    (d_inputs,) = products_call(
        inputs_kernel, (place,), (keep, got, *pairs, partial), weights, (1, 2),
        (BF,), [pltpu.VMEM((HEADS, BLOCK, 128), BF)],
    )
    (summed,) = small_call(
        gather_kernel, [terms],
        [jax.ShapeDtypeStruct((4, rows, HEADS * HEAD_DIM), F32)],
    )
    return (output[None], d_inputs[None], summed)


def solution(mesh):
    replicas = mesh.devices.shape[1]
    grid = Mesh(mesh.devices.reshape(4, 8, replicas), SEQ + ("rep",))
    return jax.shard_map(
        body,
        mesh=grid,
        in_specs=(
            P("rep", SEQ, None),
            P("rep", SEQ, None),
            P(),
            P("rep", None, None),
            P("rep", None),
        ),
        out_specs=(
            P("rep", SEQ, None),
            P("rep", SEQ, None),
            P(None, SEQ + ("rep",), None),
        ),
        check_vma=False,
    )
```

```python
import jax
import jax.numpy as jnp
from jax import lax
from jax.experimental import pallas as pl
from jax.experimental.pallas import tpu as pltpu
from jax.sharding import Mesh, PartitionSpec as P


HEADS = 8
HEAD_DIM = 64
BLOCK = 128
MAXN = 27
LARGE, SMALL = 8, 4
SLOTS = 28
BF = jnp.bfloat16
F32 = jnp.float32
INTERPRET = False


def dot(a, b):
    return jnp.dot(a, b, preferred_element_type=F32)


def dot_t(a, b):
    return lax.dot_general(a, b, (((1,), (1,)), ((), ())), preferred_element_type=F32)


def grant(mib):
    return pltpu.CompilerParams(vmem_limit_bytes=mib << 20)


def vmem(count):
    return [pl.BlockSpec(memory_space=pltpu.VMEM) for _ in range(count)]


def hbm(count):
    return [pl.BlockSpec(memory_space=pltpu.HBM) for _ in range(count)]


def position(high, low):
    return low * 8 + high


def by_head(rows, out_ref):
    for head in range(HEADS):
        cols = slice(head * HEAD_DIM, (head + 1) * HEAD_DIM)
        out_ref[head] = jnp.concatenate([rows[0, :, cols], rows[1, :, cols]], axis=1)


def keys_kernel(tok_ref, w_ref, kv_ref, rows):
    step = pl.program_id(0)
    rows[step] = dot(tok_ref[...], w_ref[0]).astype(BF)

    @pl.when(step == 1)
    def _():
        by_head(rows, kv_ref)


def queries_kernel(tok_ref, cot_ref, w_ref, qd_ref, xt_ref, rows):
    step = pl.program_id(0)

    @pl.when(step == 0)
    def _():
        queries = dot(tok_ref[...], w_ref[0]).astype(BF)
        rows[0] = (queries.astype(F32) * 0.125).astype(BF)
        xt_ref[0] = tok_ref[...].T

    @pl.when(step == 1)
    def _():
        rows[1] = dot(cot_ref[...], w_ref[0]).astype(BF)
        xt_ref[1] = cot_ref[...].T
        by_head(rows, qd_ref)


def project(kernel, arrays, weights, pick, outs):
    rows, width = arrays[0].shape
    return pl.pallas_call(
        kernel,
        grid=(2,),
        in_specs=[pl.BlockSpec((rows, width), lambda step: (0, 0)) for _ in arrays]
        + [pl.BlockSpec((1, width, HEADS * HEAD_DIM), lambda step: (pick(step), 0, 0))],
        out_specs=[pl.BlockSpec(out, lambda step: (0, 0, 0)) for out in outs],
        out_shape=[jax.ShapeDtypeStruct(out, BF) for out in outs],
        scratch_shapes=[pltpu.VMEM((2, rows, HEADS * HEAD_DIM), BF)],
        cost_estimate=pl.CostEstimate(
            flops=1_000_000_000, bytes_accessed=4_000_000, transcendentals=0
        ),
        compiler_params=grant(56),
        interpret=INTERPRET,
    )(*arrays, weights)


def attend_kernel(
    lists_ref, counts_ref, group_ref,
    qd_ref, kv0, kv1, kv2, kv3,
    y_ref, out0, out1, out2, out3,
    kvs, kvt, acc, s_scr, p_scr, ds_scr, n_scr, w_in, w_back, places, sems,
):
    step = pl.program_id(0)
    group = group_ref[0]
    block = position(step, group)

    @pl.when(step == 0)
    def _():
        copies = [
            pltpu.make_async_copy(ref, kvs.at[pl.ds(8 * part, 8)], sems.at[part])
            for part, ref in enumerate((kv0, kv1, kv2, kv3))
        ]
        for copy in copies:
            copy.start()
        acc[...] = jnp.zeros_like(acc)
        for part, copy in enumerate(copies):
            copy.wait()
            for idx in range(8 * part, 8 * part + 8):
                kvt[idx] = kvs[idx].T

    count = counts_ref[block]
    large = (count + SMALL - 1) // LARGE
    small = (count - large * LARGE + SMALL - 1) // SMALL

    def sweep(visit, carry):
        carry = lax.fori_loop(0, large, lambda i, c: visit(LARGE, i * LARGE, c), carry)
        return lax.fori_loop(
            0, small, lambda i, c: visit(SMALL, large * LARGE + i * SMALL, c), carry
        )

    def place(slot):
        raw = lists_ref[block, jnp.minimum(slot, MAXN - 1)]
        raw = jnp.where(slot < count, raw, block)
        where = raw ^ (group * 8)
        places[slot] = where
        return where

    qd = qd_ref[0]
    qdt = qd.T
    upper = lax.broadcasted_iota(jnp.int32, (128, 128), 0) < HEAD_DIM
    left = lax.broadcasted_iota(jnp.int32, (128, 128), 1) < HEAD_DIM
    zero = jnp.zeros((128, 128), BF)
    w_in[:, :128] = jnp.where(upper, qdt, zero)
    w_in[:, 128:] = jnp.where(upper, zero, qdt)
    w_back[:128] = jnp.where(left, qd, zero)
    w_back[128:] = jnp.where(left, zero, qd)

    def rows_of(slot, size):
        return pl.ds(pl.multiple_of(slot * 128, 128), size * 128)

    def scores(size, slot, top):
        stack = jnp.concatenate([kvs[place(slot + i)] for i in range(size)], axis=0)
        both = dot(stack, w_in[...])
        s_scr[rows_of(slot, size), :] = both[:, :128]
        p_scr[rows_of(slot, size), :] = both[:, 128:]
        return jnp.maximum(top, jnp.max(both[:, :128].reshape(size * 16, 8, 128), axis=0))

    top = sweep(scores, jnp.full((8, 128), -3e38, F32))
    row_max = jnp.max(top, axis=0, keepdims=True)

    def mix(size, slot, carry):
        total, mixed = carry
        parts, values = [], []
        for i in range(size):
            shift = jnp.where(slot + i < count, row_max, 1e30)
            e = jnp.exp(s_scr[rows_of(slot + i, 1), :] - shift)
            s_scr[rows_of(slot + i, 1), :] = e
            total = total + jnp.sum(e.reshape(16, 8, 128), axis=0)
            parts.append(e.astype(BF))
            values.append(kvt[places[slot + i], HEAD_DIM:, :])
        mixed = mixed + dot(jnp.concatenate(values, axis=1), jnp.concatenate(parts, axis=0))
        return total, mixed

    total, mixed = sweep(mix, (jnp.zeros((8, 128), F32), jnp.zeros((HEAD_DIM, 128), F32)))
    inverse = 1.0 / jnp.sum(total, axis=0, keepdims=True)
    attended = (mixed * inverse).astype(BF)
    delta = jnp.sum(
        qdt[HEAD_DIM:, :].astype(F32) * attended.astype(F32), axis=0, keepdims=True
    )

    def back(size, slot, dq):
        keys = []
        for i in range(size):
            rows, here = rows_of(slot + i, 1), slice(i * 128, (i + 1) * 128)
            normed = s_scr[rows, :] * inverse
            ds_scr[here, :] = (normed * (p_scr[rows, :] - delta)).astype(BF)
            n_scr[here, :] = normed.astype(BF)
            keys.append(kvt[places[slot + i], :HEAD_DIM, :])
        span = slice(0, size * 128)
        dq = dq + dot(jnp.concatenate(keys, axis=1), ds_scr[span, :])
        grads = dot(jnp.concatenate([ds_scr[span, :], n_scr[span, :]], axis=1), w_back[...])
        for i in range(size):
            acc[places[slot + i]] += grads[i * 128 : (i + 1) * 128]
        return dq

    dq = sweep(back, jnp.zeros((HEAD_DIM, 128), F32))
    y_ref[0] = jnp.concatenate([dq * 0.125, attended.astype(F32)], axis=0).T.astype(BF)

    @pl.when(step == 7)
    def _():
        for part, ref in enumerate((out0, out1, out2, out3)):
            for idx in range(8):
                ref[idx] = acc[8 * part + idx].astype(ref.dtype)


def attend(lists, counts, group, qd, kvs):
    whole3 = lambda step, *_: (0, 0, 0)
    piece = pl.BlockSpec((8, 128, 128), whole3)
    each = pl.BlockSpec((1, 128, 128), lambda step, *_: (step, 0, 0))
    shape = lambda dtype: jax.ShapeDtypeStruct((8, 128, 128), dtype)
    return pl.pallas_call(
        attend_kernel,
        grid_spec=pltpu.PrefetchScalarGridSpec(
            num_scalar_prefetch=3,
            grid=(8,),
            in_specs=[each] + hbm(4),
            out_specs=[each] + [piece] * 4,
            scratch_shapes=[
                pltpu.VMEM((32, 128, 128), BF),
                pltpu.VMEM((32, 128, 128), BF),
                pltpu.VMEM((32, 128, 128), F32),
                pltpu.VMEM((SLOTS * 128, 128), F32),
                pltpu.VMEM((SLOTS * 128, 128), F32),
                pltpu.VMEM((LARGE * 128, 128), BF),
                pltpu.VMEM((LARGE * 128, 128), BF),
                pltpu.VMEM((128, 256), BF),
                pltpu.VMEM((256, 128), BF),
                pltpu.SMEM((SLOTS,), jnp.int32),
                pltpu.SemaphoreType.DMA((4,)),
            ],
        ),
        out_shape=[shape(BF), shape(F32), shape(BF), shape(BF), shape(BF)],
        cost_estimate=pl.CostEstimate(
            flops=30_000_000_000, bytes_accessed=4_000_000, transcendentals=4_000_000
        ),
        compiler_params=grant(28),
        interpret=INTERPRET,
        name="attend",
    )(lists, counts, group, qd, *kvs)


def ordered(y_ref, place):
    return jnp.concatenate([y_ref[place ^ k] for k in (0, 2, 4, 6, 1, 3, 5, 7)], axis=0)


def deal(grads, group, scratch, outs):
    scratch[...] = grads
    size = outs[0].shape[0]
    for k, ref in enumerate(outs):
        rows = pl.ds(pl.multiple_of((group ^ k) * size, size), size)
        ref[...] = scratch[rows, :].astype(ref.dtype)


def first_grads_kernel(group_ref, place_ref, y_ref, *refs):
    xs, outs, scratch = refs[:8], refs[8:12], refs[12]
    y = ordered(y_ref, place_ref[0])
    tok = dot(jnp.concatenate([x[0] for x in xs], axis=1), y)
    cot = dot(jnp.concatenate([x[1] for x in xs], axis=1), y)
    left = lax.broadcasted_iota(jnp.int32, tok.shape, 1) < HEAD_DIM
    deal(jnp.where(left, tok, cot), group_ref[0], scratch, outs)


def second_grads_kernel(group_ref, place_ref, own, part1, part2, part3, *refs):
    xs, outs = refs[:8], refs[8:12]
    keep_ref, send_ref, scratch, y_ref, base, landed, sems = refs[12:]
    copies = [pltpu.make_async_copy(own, base, sems.at[0])] + [
        pltpu.make_async_copy(part, landed.at[k], sems.at[k + 1])
        for k, part in enumerate((part1, part2, part3))
    ]
    for copy in copies:
        copy.start()
    for copy in copies:
        copy.wait()
    y_ref[...] = (base[...] + jnp.sum(landed[...].astype(F32), axis=0)).astype(BF)
    chip, core = place_ref[0] // 2, lax.rem(place_ref[0], 2)
    for k in range(4):
        keep_ref[k] = y_ref[(chip ^ k) * 2 + core]
        send_ref[k] = y_ref[(chip ^ k) * 2 + 1 - core]
    y = ordered(y_ref, place_ref[0])
    grads = dot(jnp.concatenate([x[0] for x in xs], axis=1), y)
    deal(grads, group_ref[0], scratch, outs)


def pair_kernel(*refs):
    total = lambda four: four[0][...] + sum(ref[...].astype(F32) for ref in four[1:])
    first, second, out_ref = total(refs[0:4]), total(refs[4:8]), refs[8]
    rows = out_ref.shape[1] // 2
    for index in range(out_ref.shape[0]):
        mine = slice(index * rows, (index + 1) * rows)
        out_ref[index] = jnp.concatenate([first[mine], second[mine]], axis=0).astype(BF)


def pack_kernel(keep_ref, got_ref, *outs):
    for k, ref in enumerate(outs):
        ref[0] = keep_ref[k + 1]
        ref[1] = got_ref[k + 1]


def grads_call(kernel, scalars, specs, operands, width, more=(), scratch=()):
    quarter = lambda dtype: jax.ShapeDtypeStruct((width // 4, 128), dtype)
    outs = [quarter(F32)] + [quarter(BF)] * 3 + list(more)
    return pl.pallas_call(
        kernel,
        in_specs=[pl.BlockSpec(memory_space=pltpu.SMEM) for _ in scalars] + specs,
        out_specs=vmem(len(outs)),
        out_shape=outs,
        scratch_shapes=[pltpu.VMEM((width, 128), F32)] + list(scratch),
        cost_estimate=pl.CostEstimate(
            flops=2_000_000_000, bytes_accessed=4_000_000, transcendentals=0
        ),
        compiler_params=grant(16),
        interpret=INTERPRET,
    )(*scalars, *operands)


def gather_kernel(in_ref, out_ref):
    replicas, rows = in_ref.shape[0] // HEADS, in_ref.shape[1] // 2
    parts = [
        jnp.sum(in_ref[head * replicas : (head + 1) * replicas].astype(F32), axis=0)
        for head in range(HEADS)
    ]
    for half, (near, far) in enumerate(((0, 3), (1, 2))):
        mine = slice(half * rows, (half + 1) * rows)
        out_ref[near] = jnp.concatenate([p[mine, :HEAD_DIM] for p in parts], axis=1)
        out_ref[far] = jnp.concatenate([p[mine, HEAD_DIM:] for p in parts], axis=1)


def small_call(kernel, operands, outs):
    return pl.pallas_call(
        kernel,
        in_specs=vmem(len(operands)),
        out_specs=vmem(len(outs)),
        out_shape=outs,
        compiler_params=grant(4),
        interpret=INTERPRET,
    )(*operands)


def halves(pieces):
    first = jnp.concatenate([piece[:, :HEAD_DIM] for piece in pieces], axis=1)
    second = jnp.concatenate([piece[:, HEAD_DIM:] for piece in pieces], axis=1)
    return first, second


def output_kernel(y_ref, wq_ref, wo_ref, out_ref, part_ref):
    dq, attended = halves([y_ref[head] for head in range(HEADS)])
    out_ref[...] = dot_t(attended, wo_ref[0]).astype(BF)
    part_ref[...] = dot_t(dq, wq_ref[0])


def inputs_kernel(place_ref, keep_ref, got_ref, *refs):
    pairs, (part_ref, wk_ref, wv_ref, out_ref, heads) = refs[:3], refs[3:]
    place = place_ref[0]
    heads[place] = keep_ref[0]
    heads[place ^ 1] = got_ref[0]
    for k, pair in enumerate(pairs):
        heads[place ^ (2 * k + 2)] = pair[0]
        heads[place ^ (2 * k + 3)] = pair[1]
    dk, dv = halves([heads[head] for head in range(HEADS)])
    out_ref[...] = (part_ref[...] + dot_t(dk, wk_ref[0]) + dot_t(dv, wv_ref[0])).astype(BF)


def products_call(kernel, place, arrays, weights, picks, outs, scratch=()):
    whole = lambda array: pl.BlockSpec(array.shape, lambda step: (0,) * array.ndim)
    width = weights.shape[1]
    pick = lambda m: pl.BlockSpec((1, width, HEADS * HEAD_DIM), lambda step: (m, 0, 0))
    return pl.pallas_call(
        kernel,
        grid=(1,),
        in_specs=[pl.BlockSpec(memory_space=pltpu.SMEM) for _ in place]
        + [whole(array) for array in arrays]
        + [pick(m) for m in picks],
        out_specs=[pl.BlockSpec((BLOCK, width), lambda step: (0, 0)) for _ in outs],
        out_shape=[jax.ShapeDtypeStruct((BLOCK, width), dtype) for dtype in outs],
        scratch_shapes=list(scratch),
        cost_estimate=pl.CostEstimate(
            flops=500_000_000, bytes_accessed=4_000_000, transcendentals=0
        ),
        compiler_params=grant(12),
        interpret=INTERPRET,
    )(*place, *arrays, *[weights for _ in picks])


ROW = ("row",)
HEAD = ("head",)
SEQ = ROW + HEAD


def across(array, axes, flip):
    return lax.ppermute(array, axes, [(i, i ^ flip) for i in range(lax.axis_size(axes))])


def body(tokens, cotangent, weights, neighbour_lists, neighbour_counts):
    width = tokens.shape[2]
    rows = width // (32 * lax.axis_size("rep"))
    group = lax.axis_index(ROW).astype(jnp.int32).reshape(1)
    place = lax.axis_index(HEAD).astype(jnp.int32).reshape(1)
    swap = lambda array: lax.all_to_all(array, HEAD, 0, 0, tiled=True)
    (kv,) = project(
        keys_kernel, [tokens[0]], weights, lambda step: step + 1, [(HEADS, BLOCK, 128)]
    )
    kv = swap(kv)
    qd, xt = project(
        queries_kernel, [tokens[0], cotangent[0]], weights,
        lambda step: 3 * step, [(HEADS, BLOCK, 128), (2, width, BLOCK)],
    )
    qd, xt, kv = lax.optimization_barrier((qd, xt, kv))
    kvs = [kv] + [across(kv, ROW, k) for k in (1, 2, 3)]
    qd = swap(qd)
    xs = [xt] + [across(xt, HEAD, k) for k in (2, 4, 6)]
    y, *parts = attend(neighbour_lists[0], neighbour_counts[0], group, qd, kvs)
    xs, y = lax.optimization_barrier((xs, y))
    xs = xs + [across(x, HEAD, 1) for x in xs]
    parts = [parts[0]] + [across(parts[k], ROW, k) for k in (1, 2, 3)]
    home = swap(y)
    first = grads_call(first_grads_kernel, (group, place), vmem(9), [y, *xs], width)
    first = [first[0]] + [across(first[k], ROW, k) for k in (1, 2, 3)]
    parts, first = lax.optimization_barrier((parts, first))
    output, partial = products_call(
        output_kernel, (), (home,), weights, (0, 3), (BF, F32)
    )
    pieces = lambda count: jax.ShapeDtypeStruct((count, 128, 128), BF)
    *second, keep, send = grads_call(
        second_grads_kernel, (group, place), hbm(4) + vmem(8),
        [*parts, *xs], width, [pieces(4), pieces(4)],
        [
            pltpu.VMEM((8, 128, 128), BF),
            pltpu.VMEM((8, 128, 128), F32),
            pltpu.VMEM((3, 8, 128, 128), BF),
            pltpu.SemaphoreType.DMA((4,)),
        ],
    )
    second = second[:1] + [across(second[k], ROW, k) for k in (1, 2, 3)]
    got = across(send, HEAD, 1)
    pairs = small_call(pack_kernel, [keep, got], [pieces(2)] * 3)
    second, pairs = lax.optimization_barrier((second, pairs))
    (terms,) = small_call(
        pair_kernel, [*first, *second],
        [jax.ShapeDtypeStruct((width // 4 // rows, 2 * rows, 128), BF)],
    )
    terms = lax.all_to_all(terms, HEAD + ("rep",), 0, 0, tiled=True)
    pairs = [across(pair, HEAD, 2 * k + 2) for k, pair in enumerate(pairs)]
    (d_inputs,) = products_call(
        inputs_kernel, (place,), (keep, got, *pairs, partial), weights, (1, 2),
        (BF,), [pltpu.VMEM((HEADS, BLOCK, 128), BF)],
    )
    (summed,) = small_call(
        gather_kernel, [terms],
        [jax.ShapeDtypeStruct((4, rows, HEADS * HEAD_DIM), F32)],
    )
    return (output[None], d_inputs[None], summed)


def solution(mesh):
    replicas = mesh.devices.shape[1]
    grid = Mesh(mesh.devices.reshape(4, 8, replicas), SEQ + ("rep",))
    return jax.shard_map(
        body,
        mesh=grid,
        in_specs=(
            P("rep", SEQ, None),
            P("rep", SEQ, None),
            P(),
            P("rep", None, None),
            P("rep", None),
        ),
        out_specs=(
            P("rep", SEQ, None),
            P("rep", SEQ, None),
            P(None, SEQ + ("rep",), None),
        ),
        check_vma=False,
    )
```

```python
import jax
import jax.numpy as jnp
from jax import lax
from jax.experimental import pallas as pl
from jax.experimental.pallas import tpu as pltpu
from jax.sharding import Mesh, PartitionSpec as P


HEADS = 8
HEAD_DIM = 64
BLOCK = 128
MAXN = 27
LARGE, SMALL = 8, 4
SLOTS = 28
BF = jnp.bfloat16
F32 = jnp.float32
INTERPRET = False


def dot(a, b):
    return jnp.dot(a, b, preferred_element_type=F32)


def dot_t(a, b):
    return lax.dot_general(a, b, (((1,), (1,)), ((), ())), preferred_element_type=F32)


def grant(mib):
    return pltpu.CompilerParams(vmem_limit_bytes=mib << 20)


def vmem(count):
    return [pl.BlockSpec(memory_space=pltpu.VMEM) for _ in range(count)]


def hbm(count):
    return [pl.BlockSpec(memory_space=pltpu.HBM) for _ in range(count)]


def position(high, low):
    return low * 8 + high


def by_head(rows, out_ref):
    for head in range(HEADS):
        cols = slice(head * HEAD_DIM, (head + 1) * HEAD_DIM)
        out_ref[head] = jnp.concatenate([rows[0, :, cols], rows[1, :, cols]], axis=1)


def keys_kernel(tok_ref, w_ref, kv_ref, rows):
    step = pl.program_id(0)
    rows[step] = dot(tok_ref[...], w_ref[0]).astype(BF)

    @pl.when(step == 1)
    def _():
        by_head(rows, kv_ref)


def queries_kernel(tok_ref, cot_ref, w_ref, qd_ref, xt_ref, rows):
    step = pl.program_id(0)

    @pl.when(step == 0)
    def _():
        queries = dot(tok_ref[...], w_ref[0]).astype(BF)
        rows[0] = (queries.astype(F32) * 0.125).astype(BF)
        xt_ref[0] = tok_ref[...].T

    @pl.when(step == 1)
    def _():
        rows[1] = dot(cot_ref[...], w_ref[0]).astype(BF)
        xt_ref[1] = cot_ref[...].T
        by_head(rows, qd_ref)


def project(kernel, arrays, weights, pick, outs):
    rows, width = arrays[0].shape
    return pl.pallas_call(
        kernel,
        grid=(2,),
        in_specs=[pl.BlockSpec((rows, width), lambda step: (0, 0)) for _ in arrays]
        + [pl.BlockSpec((1, width, HEADS * HEAD_DIM), lambda step: (pick(step), 0, 0))],
        out_specs=[pl.BlockSpec(out, lambda step: (0, 0, 0)) for out in outs],
        out_shape=[jax.ShapeDtypeStruct(out, BF) for out in outs],
        scratch_shapes=[pltpu.VMEM((2, rows, HEADS * HEAD_DIM), BF)],
        cost_estimate=pl.CostEstimate(
            flops=1_000_000_000, bytes_accessed=4_000_000, transcendentals=0
        ),
        compiler_params=grant(56),
        interpret=INTERPRET,
    )(*arrays, weights)


def attend_kernel(
    lists_ref, counts_ref, group_ref,
    qd_ref, kv0, kv1, kv2, kv3,
    y_ref, out0, out1, out2, out3,
    kvs, kvt, acc, s_scr, p_scr, ds_scr, n_scr, w_in, w_back, places, sems,
):
    step = pl.program_id(0)
    group = group_ref[0]
    block = position(step, group)

    @pl.when(step == 0)
    def _():
        copies = [
            pltpu.make_async_copy(ref, kvs.at[pl.ds(8 * part, 8)], sems.at[part])
            for part, ref in enumerate((kv0, kv1, kv2, kv3))
        ]
        for copy in copies:
            copy.start()
        acc[...] = jnp.zeros_like(acc)
        for part, copy in enumerate(copies):
            copy.wait()
            for idx in range(8 * part, 8 * part + 8):
                kvt[idx] = kvs[idx].T

    count = counts_ref[block]
    large = (count + SMALL - 1) // LARGE
    small = (count - large * LARGE + SMALL - 1) // SMALL

    def sweep(visit, carry):
        carry = lax.fori_loop(0, large, lambda i, c: visit(LARGE, i * LARGE, c), carry)
        return lax.fori_loop(
            0, small, lambda i, c: visit(SMALL, large * LARGE + i * SMALL, c), carry
        )

    def place(slot):
        raw = lists_ref[block, jnp.minimum(slot, MAXN - 1)]
        raw = jnp.where(slot < count, raw, block)
        where = raw ^ (group * 8)
        places[slot] = where
        return where

    qd = qd_ref[0]
    qdt = qd.T
    upper = lax.broadcasted_iota(jnp.int32, (128, 128), 0) < HEAD_DIM
    left = lax.broadcasted_iota(jnp.int32, (128, 128), 1) < HEAD_DIM
    zero = jnp.zeros((128, 128), BF)
    w_in[:, :128] = jnp.where(upper, qdt, zero)
    w_in[:, 128:] = jnp.where(upper, zero, qdt)
    w_back[:128] = jnp.where(left, qd, zero)
    w_back[128:] = jnp.where(left, zero, qd)

    def rows_of(slot, size):
        return pl.ds(pl.multiple_of(slot * 128, 128), size * 128)

    def scores(size, slot, top):
        stack = jnp.concatenate([kvs[place(slot + i)] for i in range(size)], axis=0)
        both = dot(stack, w_in[...])
        s_scr[rows_of(slot, size), :] = both[:, :128]
        p_scr[rows_of(slot, size), :] = both[:, 128:]
        return jnp.maximum(top, jnp.max(both[:, :128].reshape(size * 16, 8, 128), axis=0))

    top = sweep(scores, jnp.full((8, 128), -3e38, F32))
    row_max = jnp.max(top, axis=0, keepdims=True)

    def mix(size, slot, carry):
        total, mixed = carry
        parts, values = [], []
        for i in range(size):
            shift = jnp.where(slot + i < count, row_max, 1e30)
            e = jnp.exp(s_scr[rows_of(slot + i, 1), :] - shift)
            s_scr[rows_of(slot + i, 1), :] = e
            total = total + jnp.sum(e.reshape(16, 8, 128), axis=0)
            parts.append(e.astype(BF))
            values.append(kvt[places[slot + i], HEAD_DIM:, :])
        mixed = mixed + dot(jnp.concatenate(values, axis=1), jnp.concatenate(parts, axis=0))
        return total, mixed

    total, mixed = sweep(mix, (jnp.zeros((8, 128), F32), jnp.zeros((HEAD_DIM, 128), F32)))
    inverse = 1.0 / jnp.sum(total, axis=0, keepdims=True)
    attended = (mixed * inverse).astype(BF)
    delta = jnp.sum(
        qdt[HEAD_DIM:, :].astype(F32) * attended.astype(F32), axis=0, keepdims=True
    )

    def back(size, slot, dq):
        keys = []
        for i in range(size):
            rows, here = rows_of(slot + i, 1), slice(i * 128, (i + 1) * 128)
            normed = s_scr[rows, :] * inverse
            ds_scr[here, :] = (normed * (p_scr[rows, :] - delta)).astype(BF)
            n_scr[here, :] = normed.astype(BF)
            keys.append(kvt[places[slot + i], :HEAD_DIM, :])
        span = slice(0, size * 128)
        dq = dq + dot(jnp.concatenate(keys, axis=1), ds_scr[span, :])
        grads = dot(jnp.concatenate([ds_scr[span, :], n_scr[span, :]], axis=1), w_back[...])
        for i in range(size):
            acc[places[slot + i]] += grads[i * 128 : (i + 1) * 128]
        return dq

    dq = sweep(back, jnp.zeros((HEAD_DIM, 128), F32))
    y_ref[0] = jnp.concatenate([dq * 0.125, attended.astype(F32)], axis=0).T.astype(BF)

    @pl.when(step == 7)
    def _():
        for part, ref in enumerate((out0, out1, out2, out3)):
            for idx in range(8):
                ref[idx] = acc[8 * part + idx].astype(ref.dtype)


def attend(lists, counts, group, qd, kvs):
    whole3 = lambda step, *_: (0, 0, 0)
    piece = pl.BlockSpec((8, 128, 128), whole3)
    each = pl.BlockSpec((1, 128, 128), lambda step, *_: (step, 0, 0))
    shape = lambda dtype: jax.ShapeDtypeStruct((8, 128, 128), dtype)
    return pl.pallas_call(
        attend_kernel,
        grid_spec=pltpu.PrefetchScalarGridSpec(
            num_scalar_prefetch=3,
            grid=(8,),
            in_specs=[each] + hbm(4),
            out_specs=[each] + [piece] * 4,
            scratch_shapes=[
                pltpu.VMEM((32, 128, 128), BF),
                pltpu.VMEM((32, 128, 128), BF),
                pltpu.VMEM((32, 128, 128), F32),
                pltpu.VMEM((SLOTS * 128, 128), F32),
                pltpu.VMEM((SLOTS * 128, 128), F32),
                pltpu.VMEM((LARGE * 128, 128), BF),
                pltpu.VMEM((LARGE * 128, 128), BF),
                pltpu.VMEM((128, 256), BF),
                pltpu.VMEM((256, 128), BF),
                pltpu.SMEM((SLOTS,), jnp.int32),
                pltpu.SemaphoreType.DMA((4,)),
            ],
        ),
        out_shape=[shape(BF), shape(F32), shape(BF), shape(BF), shape(BF)],
        cost_estimate=pl.CostEstimate(
            flops=30_000_000_000, bytes_accessed=4_000_000, transcendentals=4_000_000
        ),
        compiler_params=grant(28),
        interpret=INTERPRET,
        name="attend",
    )(lists, counts, group, qd, *kvs)


def ordered(y_ref, place):
    return jnp.concatenate([y_ref[place ^ k] for k in (0, 2, 4, 6, 1, 3, 5, 7)], axis=0)


def first_grads_kernel(place_ref, y_ref, *refs):
    xs, out_ref = refs[:8], refs[8]
    y = ordered(y_ref, place_ref[0])
    tok = dot(jnp.concatenate([x[0] for x in xs], axis=1), y)
    cot = dot(jnp.concatenate([x[1] for x in xs], axis=1), y)
    left = lax.broadcasted_iota(jnp.int32, tok.shape, 1) < HEAD_DIM
    out_ref[...] = jnp.where(left, tok, cot)


def second_grads_kernel(place_ref, own, part1, part2, part3, first_ref, *refs):
    xs, (out_ref, keep_ref, send_ref, y_ref, base, landed, sems) = refs[:8], refs[8:]
    copies = [pltpu.make_async_copy(own, base, sems.at[0])] + [
        pltpu.make_async_copy(part, landed.at[k], sems.at[k + 1])
        for k, part in enumerate((part1, part2, part3))
    ]
    for copy in copies:
        copy.start()
    for copy in copies:
        copy.wait()
    y_ref[...] = (base[...] + jnp.sum(landed[...].astype(F32), axis=0)).astype(BF)
    chip, core = place_ref[0] // 2, lax.rem(place_ref[0], 2)
    for k in range(4):
        keep_ref[k] = y_ref[(chip ^ k) * 2 + core]
        send_ref[k] = y_ref[(chip ^ k) * 2 + 1 - core]
    y = ordered(y_ref, place_ref[0])
    second = dot(jnp.concatenate([x[0] for x in xs], axis=1), y)
    rows = out_ref.shape[1] // 2
    for index in range(out_ref.shape[0]):
        mine = slice(index * rows, (index + 1) * rows)
        out_ref[index] = jnp.concatenate([first_ref[mine], second[mine]], axis=0).astype(BF)


def pack_kernel(keep_ref, got_ref, *outs):
    for k, ref in enumerate(outs):
        ref[0] = keep_ref[k + 1]
        ref[1] = got_ref[k + 1]


def grads_call(kernel, place, specs, operands, outs, scratch=()):
    return pl.pallas_call(
        kernel,
        in_specs=[pl.BlockSpec(memory_space=pltpu.SMEM)] + specs,
        out_specs=vmem(len(outs)),
        out_shape=outs,
        scratch_shapes=list(scratch),
        cost_estimate=pl.CostEstimate(
            flops=2_000_000_000, bytes_accessed=4_000_000, transcendentals=0
        ),
        compiler_params=grant(16),
        interpret=INTERPRET,
    )(place, *operands)


def gather_kernel(in_ref, out_ref):
    replicas, rows = in_ref.shape[0] // 32, in_ref.shape[1] // 2
    parts = []
    for head in range(HEADS):
        total = None
        for low in range(4):
            start = position(head, low) * replicas
            term = jnp.sum(in_ref[start : start + replicas].astype(F32), axis=0)
            total = term if total is None else total + term
        parts.append(total)
    for half, (near, far) in enumerate(((0, 3), (1, 2))):
        mine = slice(half * rows, (half + 1) * rows)
        out_ref[near] = jnp.concatenate([p[mine, :HEAD_DIM] for p in parts], axis=1)
        out_ref[far] = jnp.concatenate([p[mine, HEAD_DIM:] for p in parts], axis=1)


def small_call(kernel, operands, outs):
    return pl.pallas_call(
        kernel,
        in_specs=vmem(len(operands)),
        out_specs=vmem(len(outs)),
        out_shape=outs,
        compiler_params=grant(4),
        interpret=INTERPRET,
    )(*operands)


def halves(pieces):
    first = jnp.concatenate([piece[:, :HEAD_DIM] for piece in pieces], axis=1)
    second = jnp.concatenate([piece[:, HEAD_DIM:] for piece in pieces], axis=1)
    return first, second


def output_kernel(y_ref, wq_ref, wo_ref, out_ref, part_ref):
    dq, attended = halves([y_ref[head] for head in range(HEADS)])
    out_ref[...] = dot_t(attended, wo_ref[0]).astype(BF)
    part_ref[...] = dot_t(dq, wq_ref[0])


def inputs_kernel(place_ref, keep_ref, got_ref, *refs):
    pairs, (part_ref, wk_ref, wv_ref, out_ref, heads) = refs[:3], refs[3:]
    place = place_ref[0]
    heads[place] = keep_ref[0]
    heads[place ^ 1] = got_ref[0]
    for k, pair in enumerate(pairs):
        heads[place ^ (2 * k + 2)] = pair[0]
        heads[place ^ (2 * k + 3)] = pair[1]
    dk, dv = halves([heads[head] for head in range(HEADS)])
    out_ref[...] = (part_ref[...] + dot_t(dk, wk_ref[0]) + dot_t(dv, wv_ref[0])).astype(BF)


def products_call(kernel, place, arrays, weights, picks, outs, scratch=()):
    whole = lambda array: pl.BlockSpec(array.shape, lambda step: (0,) * array.ndim)
    width = weights.shape[1]
    pick = lambda m: pl.BlockSpec((1, width, HEADS * HEAD_DIM), lambda step: (m, 0, 0))
    return pl.pallas_call(
        kernel,
        grid=(1,),
        in_specs=[pl.BlockSpec(memory_space=pltpu.SMEM) for _ in place]
        + [whole(array) for array in arrays]
        + [pick(m) for m in picks],
        out_specs=[pl.BlockSpec((BLOCK, width), lambda step: (0, 0)) for _ in outs],
        out_shape=[jax.ShapeDtypeStruct((BLOCK, width), dtype) for dtype in outs],
        scratch_shapes=list(scratch),
        cost_estimate=pl.CostEstimate(
            flops=500_000_000, bytes_accessed=4_000_000, transcendentals=0
        ),
        compiler_params=grant(12),
        interpret=INTERPRET,
    )(*place, *arrays, *[weights for _ in picks])


ROW = ("row",)
HEAD = ("head",)
SEQ = ROW + HEAD


def across(array, axes, flip):
    return lax.ppermute(array, axes, [(i, i ^ flip) for i in range(lax.axis_size(axes))])


def body(tokens, cotangent, weights, neighbour_lists, neighbour_counts):
    width = tokens.shape[2]
    rows = width // (32 * lax.axis_size("rep"))
    group = lax.axis_index(ROW).astype(jnp.int32).reshape(1)
    place = lax.axis_index(HEAD).astype(jnp.int32).reshape(1)
    swap = lambda array: lax.all_to_all(array, HEAD, 0, 0, tiled=True)
    (kv,) = project(keys_kernel, [tokens[0]], weights, lambda step: step + 1, [(HEADS, BLOCK, 128)])
    kv = swap(kv)
    qd, xt = project(
        queries_kernel, [tokens[0], cotangent[0]], weights,
        lambda step: 3 * step, [(HEADS, BLOCK, 128), (2, width, BLOCK)],
    )
    qd, xt, kv = lax.optimization_barrier((qd, xt, kv))
    kvs = [kv] + [across(kv, ROW, k) for k in (1, 2, 3)]
    qd = swap(qd)
    xs = [xt] + [across(xt, HEAD, k) for k in (2, 4, 6)]
    y, *parts = attend(neighbour_lists[0], neighbour_counts[0], group, qd, kvs)
    xs, y = lax.optimization_barrier((xs, y))
    xs = xs + [across(x, HEAD, 1) for x in xs]
    parts = [parts[0]] + [across(parts[k], ROW, k) for k in (1, 2, 3)]
    home = swap(y)
    (first,) = grads_call(
        first_grads_kernel, place, vmem(9), [y, *xs],
        [jax.ShapeDtypeStruct((width, 128), F32)],
    )
    output, partial = products_call(output_kernel, (), (home,), weights, (0, 3), (BF, F32))
    pieces = lambda count: jax.ShapeDtypeStruct((count, 128, 128), BF)
    terms, keep, send = grads_call(
        second_grads_kernel, place, hbm(4) + vmem(9),
        [*parts, first, *xs],
        [jax.ShapeDtypeStruct((width // rows, 2 * rows, 128), BF), pieces(4), pieces(4)],
        [
            pltpu.VMEM((8, 128, 128), BF),
            pltpu.VMEM((8, 128, 128), F32),
            pltpu.VMEM((3, 8, 128, 128), BF),
            pltpu.SemaphoreType.DMA((4,)),
        ],
    )
    terms = lax.all_to_all(terms, SEQ + ("rep",), 0, 0, tiled=True)
    got = across(send, HEAD, 1)
    pairs = small_call(pack_kernel, [keep, got], [pieces(2)] * 3)
    pairs = [across(pair, HEAD, 2 * k + 2) for k, pair in enumerate(pairs)]
    (d_inputs,) = products_call(
        inputs_kernel, (place,), (keep, got, *pairs, partial), weights, (1, 2),
        (BF,), [pltpu.VMEM((HEADS, BLOCK, 128), BF)],
    )
    (summed,) = small_call(
        gather_kernel, [terms],
        [jax.ShapeDtypeStruct((4, rows, HEADS * HEAD_DIM), F32)],
    )
    return (output[None], d_inputs[None], summed)


def solution(mesh):
    replicas = mesh.devices.shape[1]
    grid = Mesh(mesh.devices.reshape(4, 8, replicas), SEQ + ("rep",))
    return jax.shard_map(
        body,
        mesh=grid,
        in_specs=(
            P("rep", SEQ, None),
            P("rep", SEQ, None),
            P(),
            P("rep", None, None),
            P("rep", None),
        ),
        out_specs=(
            P("rep", SEQ, None),
            P("rep", SEQ, None),
            P(None, SEQ + ("rep",), None),
        ),
        check_vma=False,
    )
```

```python
import jax
import jax.numpy as jnp
from jax import lax
from jax.experimental import pallas as pl
from jax.experimental.pallas import tpu as pltpu
from jax.sharding import Mesh, PartitionSpec as P


HEADS = 8
HEAD_DIM = 64
BLOCK = 128
MAXN = 27
LARGE = 8
SLOTS = 28
BF = jnp.bfloat16
F32 = jnp.float32
INTERPRET = False


def dot(a, b):
    return jnp.dot(a, b, preferred_element_type=F32)


def dot_t(a, b):
    return lax.dot_general(a, b, (((1,), (1,)), ((), ())), preferred_element_type=F32)


def grant(mib):
    return pltpu.CompilerParams(vmem_limit_bytes=mib << 20)


def vmem(count):
    return [pl.BlockSpec(memory_space=pltpu.VMEM) for _ in range(count)]


def hbm(count):
    return [pl.BlockSpec(memory_space=pltpu.HBM) for _ in range(count)]


def position(high, low):
    return low * 8 + high


def by_head(rows, out_ref):
    for head in range(HEADS):
        cols = slice(head * HEAD_DIM, (head + 1) * HEAD_DIM)
        out_ref[head] = jnp.concatenate([rows[0, :, cols], rows[1, :, cols]], axis=1)


def keys_kernel(tok_ref, w_ref, kv_ref, rows):
    step, part = pl.program_id(0), pl.program_id(1)
    size = w_ref.shape[2]
    cols = pl.ds(pl.multiple_of(part * size, size), size)
    rows[step, :, cols] = dot(tok_ref[...], w_ref[0]).astype(BF)

    @pl.when((step == 1) & (part == pl.num_programs(1) - 1))
    def _():
        by_head(rows, kv_ref)


def queries_kernel(tok_ref, cot_ref, w_ref, qd_ref, xt_ref, rows):
    step = pl.program_id(0)

    @pl.when(step == 0)
    def _():
        queries = dot(tok_ref[...], w_ref[0]).astype(BF)
        rows[0] = (queries.astype(F32) * 0.125).astype(BF)
        xt_ref[0] = tok_ref[...].T

    @pl.when(step == 1)
    def _():
        rows[1] = dot(cot_ref[...], w_ref[0]).astype(BF)
        xt_ref[1] = cot_ref[...].T
        by_head(rows, qd_ref)


def project(kernel, arrays, weights, pick, outs, cuts=1):
    rows, width = arrays[0].shape
    columns = HEADS * HEAD_DIM
    return pl.pallas_call(
        kernel,
        grid=(2, cuts),
        in_specs=[pl.BlockSpec((rows, width), lambda step, part: (0, 0)) for _ in arrays]
        + [pl.BlockSpec((1, width, columns // cuts), lambda step, part: (pick(step), 0, part))],
        out_specs=[pl.BlockSpec(out, lambda step, part: (0, 0, 0)) for out in outs],
        out_shape=[jax.ShapeDtypeStruct(out, BF) for out in outs],
        scratch_shapes=[pltpu.VMEM((2, rows, columns), BF)],
        cost_estimate=pl.CostEstimate(
            flops=1_000_000_000, bytes_accessed=4_000_000, transcendentals=0
        ),
        compiler_params=grant(56),
        interpret=INTERPRET,
    )(*arrays, weights)


def attend_kernel(
    lists_ref, counts_ref, group_ref,
    qd_ref, kv0, kv1, kv2, kv3,
    y_ref, out0, out1, out2, out3,
    kvs, kvt, acc, s_scr, p_scr, ds_scr, n_scr, w_in, w_back, places, sems,
):
    step = pl.program_id(0)
    group = group_ref[0]
    block = position(step, group)

    @pl.when(step == 0)
    def _():
        copies = [
            pltpu.make_async_copy(ref, kvs.at[pl.ds(8 * part, 8)], sems.at[part])
            for part, ref in enumerate((kv0, kv1, kv2, kv3))
        ]
        for copy in copies:
            copy.start()
        acc[...] = jnp.zeros_like(acc)
        for part, copy in enumerate(copies):
            copy.wait()
            for idx in range(8 * part, 8 * part + 8):
                kvt[idx] = kvs[idx].T

    count = counts_ref[block]
    eights = (count + 1) // 8
    rest = count - eights * 8
    fours = (rest + 1) // 4
    twos = (rest - fours * 4 + 1) // 2

    def sweep(visit, carry):
        after = eights * 8
        carry = lax.fori_loop(0, eights, lambda i, c: visit(8, i * 8, c), carry)
        carry = lax.fori_loop(0, fours, lambda i, c: visit(4, after + i * 4, c), carry)
        after = after + fours * 4
        return lax.fori_loop(0, twos, lambda i, c: visit(2, after + i * 2, c), carry)

    def place(slot):
        raw = lists_ref[block, jnp.minimum(slot, MAXN - 1)]
        raw = jnp.where(slot < count, raw, block)
        where = raw ^ (group * 8)
        places[slot] = where
        return where

    qd = qd_ref[0]
    qdt = qd.T
    upper = lax.broadcasted_iota(jnp.int32, (128, 128), 0) < HEAD_DIM
    left = lax.broadcasted_iota(jnp.int32, (128, 128), 1) < HEAD_DIM
    zero = jnp.zeros((128, 128), BF)
    w_in[:, :128] = jnp.where(upper, qdt, zero)
    w_in[:, 128:] = jnp.where(upper, zero, qdt)
    w_back[:128] = jnp.where(left, qd, zero)
    w_back[128:] = jnp.where(left, zero, qd)

    def rows_of(slot, size):
        return pl.ds(pl.multiple_of(slot * 128, 128), size * 128)

    def scores(size, slot, top):
        stack = jnp.concatenate([kvs[place(slot + i)] for i in range(size)], axis=0)
        both = dot(stack, w_in[...])
        s_scr[rows_of(slot, size), :] = both[:, :128]
        p_scr[rows_of(slot, size), :] = both[:, 128:]
        return jnp.maximum(top, jnp.max(both[:, :128].reshape(size * 16, 8, 128), axis=0))

    top = sweep(scores, jnp.full((8, 128), -3e38, F32))
    row_max = jnp.max(top, axis=0, keepdims=True)

    def mix(size, slot, carry):
        total, mixed = carry
        parts, values = [], []
        for i in range(size):
            shift = jnp.where(slot + i < count, row_max, 1e30)
            e = jnp.exp(s_scr[rows_of(slot + i, 1), :] - shift)
            s_scr[rows_of(slot + i, 1), :] = e
            total = total + jnp.sum(e.reshape(16, 8, 128), axis=0)
            parts.append(e.astype(BF))
            values.append(kvt[places[slot + i], HEAD_DIM:, :])
        mixed = mixed + dot(jnp.concatenate(values, axis=1), jnp.concatenate(parts, axis=0))
        return total, mixed

    total, mixed = sweep(mix, (jnp.zeros((8, 128), F32), jnp.zeros((HEAD_DIM, 128), F32)))
    inverse = 1.0 / jnp.sum(total, axis=0, keepdims=True)
    attended = (mixed * inverse).astype(BF)
    delta = jnp.sum(
        qdt[HEAD_DIM:, :].astype(F32) * attended.astype(F32), axis=0, keepdims=True
    )

    def back(size, slot, dq):
        keys = []
        for i in range(size):
            rows, here = rows_of(slot + i, 1), slice(i * 128, (i + 1) * 128)
            normed = s_scr[rows, :] * inverse
            ds_scr[here, :] = (normed * (p_scr[rows, :] - delta)).astype(BF)
            n_scr[here, :] = normed.astype(BF)
            keys.append(kvt[places[slot + i], :HEAD_DIM, :])
        span = slice(0, size * 128)
        dq = dq + dot(jnp.concatenate(keys, axis=1), ds_scr[span, :])
        grads = dot(jnp.concatenate([ds_scr[span, :], n_scr[span, :]], axis=1), w_back[...])
        for i in range(size):
            acc[places[slot + i]] += grads[i * 128 : (i + 1) * 128]
        return dq

    dq = sweep(back, jnp.zeros((HEAD_DIM, 128), F32))
    y_ref[0] = jnp.concatenate([dq * 0.125, attended.astype(F32)], axis=0).T.astype(BF)

    @pl.when(step == 7)
    def _():
        for part, ref in enumerate((out0, out1, out2, out3)):
            for idx in range(8):
                ref[idx] = acc[8 * part + idx].astype(ref.dtype)


def attend(lists, counts, group, qd, kvs):
    whole3 = lambda step, *_: (0, 0, 0)
    piece = pl.BlockSpec((8, 128, 128), whole3)
    each = pl.BlockSpec((1, 128, 128), lambda step, *_: (step, 0, 0))
    shape = lambda dtype: jax.ShapeDtypeStruct((8, 128, 128), dtype)
    return pl.pallas_call(
        attend_kernel,
        grid_spec=pltpu.PrefetchScalarGridSpec(
            num_scalar_prefetch=3,
            grid=(8,),
            in_specs=[each] + hbm(4),
            out_specs=[each] + [piece] * 4,
            scratch_shapes=[
                pltpu.VMEM((32, 128, 128), BF),
                pltpu.VMEM((32, 128, 128), BF),
                pltpu.VMEM((32, 128, 128), F32),
                pltpu.VMEM((SLOTS * 128, 128), F32),
                pltpu.VMEM((SLOTS * 128, 128), F32),
                pltpu.VMEM((LARGE * 128, 128), BF),
                pltpu.VMEM((LARGE * 128, 128), BF),
                pltpu.VMEM((128, 256), BF),
                pltpu.VMEM((256, 128), BF),
                pltpu.SMEM((SLOTS,), jnp.int32),
                pltpu.SemaphoreType.DMA((4,)),
            ],
        ),
        out_shape=[shape(BF), shape(F32), shape(BF), shape(BF), shape(BF)],
        cost_estimate=pl.CostEstimate(
            flops=30_000_000_000, bytes_accessed=4_000_000, transcendentals=4_000_000
        ),
        compiler_params=grant(28),
        interpret=INTERPRET,
        name="attend",
    )(lists, counts, group, qd, *kvs)


def ordered(y_ref, place):
    return jnp.concatenate([y_ref[place ^ k] for k in (0, 2, 4, 6, 1, 3, 5, 7)], axis=0)


def first_grads_kernel(place_ref, y_ref, *refs):
    xs, out_ref = refs[:8], refs[8]
    y = ordered(y_ref, place_ref[0])
    tok = dot(jnp.concatenate([x[0] for x in xs], axis=1), y)
    cot = dot(jnp.concatenate([x[1] for x in xs], axis=1), y)
    left = lax.broadcasted_iota(jnp.int32, tok.shape, 1) < HEAD_DIM
    out_ref[...] = jnp.where(left, tok, cot)


def second_grads_kernel(place_ref, own, part1, part2, part3, first_ref, *refs):
    xs, (out_ref, keep_ref, send_ref, y_ref, base, landed, sems) = refs[:8], refs[8:]
    copies = [pltpu.make_async_copy(own, base, sems.at[0])] + [
        pltpu.make_async_copy(part, landed.at[k], sems.at[k + 1])
        for k, part in enumerate((part1, part2, part3))
    ]
    for copy in copies:
        copy.start()
    for copy in copies:
        copy.wait()
    y_ref[...] = (base[...] + jnp.sum(landed[...].astype(F32), axis=0)).astype(BF)
    chip, core = place_ref[0] // 2, lax.rem(place_ref[0], 2)
    for k in range(4):
        keep_ref[k] = y_ref[(chip ^ k) * 2 + core]
        send_ref[k] = y_ref[(chip ^ k) * 2 + 1 - core]
    y = ordered(y_ref, place_ref[0])
    second = dot(jnp.concatenate([x[0] for x in xs], axis=1), y)
    rows = out_ref.shape[1] // 2
    for index in range(out_ref.shape[0]):
        mine = slice(index * rows, (index + 1) * rows)
        out_ref[index] = jnp.concatenate([first_ref[mine], second[mine]], axis=0).astype(BF)


def pack_kernel(keep_ref, got_ref, *outs):
    for k, ref in enumerate(outs):
        ref[0] = keep_ref[k + 1]
        ref[1] = got_ref[k + 1]


def grads_call(kernel, place, specs, operands, outs, scratch=()):
    return pl.pallas_call(
        kernel,
        in_specs=[pl.BlockSpec(memory_space=pltpu.SMEM)] + specs,
        out_specs=vmem(len(outs)),
        out_shape=outs,
        scratch_shapes=list(scratch),
        cost_estimate=pl.CostEstimate(
            flops=2_000_000_000, bytes_accessed=4_000_000, transcendentals=0
        ),
        compiler_params=grant(16),
        interpret=INTERPRET,
    )(place, *operands)


def gather_kernel(in_ref, out_ref):
    replicas, rows = in_ref.shape[0] // 32, in_ref.shape[1] // 2
    parts = []
    for head in range(HEADS):
        total = None
        for low in range(4):
            start = position(head, low) * replicas
            term = jnp.sum(in_ref[start : start + replicas].astype(F32), axis=0)
            total = term if total is None else total + term
        parts.append(total)
    for half, (near, far) in enumerate(((0, 3), (1, 2))):
        mine = slice(half * rows, (half + 1) * rows)
        out_ref[near] = jnp.concatenate([p[mine, :HEAD_DIM] for p in parts], axis=1)
        out_ref[far] = jnp.concatenate([p[mine, HEAD_DIM:] for p in parts], axis=1)


def small_call(kernel, operands, outs):
    return pl.pallas_call(
        kernel,
        in_specs=vmem(len(operands)),
        out_specs=vmem(len(outs)),
        out_shape=outs,
        compiler_params=grant(4),
        interpret=INTERPRET,
    )(*operands)


def halves(pieces):
    first = jnp.concatenate([piece[:, :HEAD_DIM] for piece in pieces], axis=1)
    second = jnp.concatenate([piece[:, HEAD_DIM:] for piece in pieces], axis=1)
    return first, second


def output_kernel(y_ref, wq_ref, wo_ref, out_ref, part_ref):
    dq, attended = halves([y_ref[head] for head in range(HEADS)])
    out_ref[...] = dot_t(attended, wo_ref[0]).astype(BF)
    part_ref[...] = dot_t(dq, wq_ref[0])


def inputs_kernel(place_ref, keep_ref, got_ref, *refs):
    pairs, (part_ref, wk_ref, wv_ref, out_ref, heads) = refs[:3], refs[3:]
    place = place_ref[0]
    heads[place] = keep_ref[0]
    heads[place ^ 1] = got_ref[0]
    for k, pair in enumerate(pairs):
        heads[place ^ (2 * k + 2)] = pair[0]
        heads[place ^ (2 * k + 3)] = pair[1]
    dk, dv = halves([heads[head] for head in range(HEADS)])
    out_ref[...] = (part_ref[...] + dot_t(dk, wk_ref[0]) + dot_t(dv, wv_ref[0])).astype(BF)


def products_call(kernel, place, arrays, weights, picks, outs, scratch=()):
    whole = lambda array: pl.BlockSpec(array.shape, lambda step: (0,) * array.ndim)
    width = weights.shape[1]
    pick = lambda m: pl.BlockSpec((1, width, HEADS * HEAD_DIM), lambda step: (m, 0, 0))
    return pl.pallas_call(
        kernel,
        grid=(1,),
        in_specs=[pl.BlockSpec(memory_space=pltpu.SMEM) for _ in place]
        + [whole(array) for array in arrays]
        + [pick(m) for m in picks],
        out_specs=[pl.BlockSpec((BLOCK, width), lambda step: (0, 0)) for _ in outs],
        out_shape=[jax.ShapeDtypeStruct((BLOCK, width), dtype) for dtype in outs],
        scratch_shapes=list(scratch),
        cost_estimate=pl.CostEstimate(
            flops=500_000_000, bytes_accessed=4_000_000, transcendentals=0
        ),
        compiler_params=grant(12),
        interpret=INTERPRET,
    )(*place, *arrays, *[weights for _ in picks])


ROW = ("row",)
HEAD = ("head",)
SEQ = ROW + HEAD


def across(array, axes, flip):
    return lax.ppermute(array, axes, [(i, i ^ flip) for i in range(lax.axis_size(axes))])


def body(tokens, cotangent, weights, neighbour_lists, neighbour_counts):
    width = tokens.shape[2]
    rows = width // (32 * lax.axis_size("rep"))
    group = lax.axis_index(ROW).astype(jnp.int32).reshape(1)
    place = lax.axis_index(HEAD).astype(jnp.int32).reshape(1)
    swap = lambda array: lax.all_to_all(array, HEAD, 0, 0, tiled=True)
    (kv,) = project(
        keys_kernel, [tokens[0]], weights, lambda step: step + 1,
        [(HEADS, BLOCK, 128)], 2,
    )
    kv = swap(kv)
    qd, xt = project(
        queries_kernel, [tokens[0], cotangent[0]], weights,
        lambda step: 3 * step, [(HEADS, BLOCK, 128), (2, width, BLOCK)],
    )
    qd, xt, kv = lax.optimization_barrier((qd, xt, kv))
    kvs = [kv] + [across(kv, ROW, k) for k in (1, 2, 3)]
    qd = swap(qd)
    xs = [xt] + [across(xt, HEAD, k) for k in (2, 4, 6)]
    y, *parts = attend(neighbour_lists[0], neighbour_counts[0], group, qd, kvs)
    xs, y = lax.optimization_barrier((xs, y))
    xs = xs + [across(x, HEAD, 1) for x in xs]
    parts = [parts[0]] + [across(parts[k], ROW, k) for k in (1, 2, 3)]
    home = swap(y)
    (first,) = grads_call(
        first_grads_kernel, place, vmem(9), [y, *xs],
        [jax.ShapeDtypeStruct((width, 128), F32)],
    )
    output, partial = products_call(output_kernel, (), (home,), weights, (0, 3), (BF, F32))
    pieces = lambda count: jax.ShapeDtypeStruct((count, 128, 128), BF)
    terms, keep, send = grads_call(
        second_grads_kernel, place, hbm(4) + vmem(9),
        [*parts, first, *xs],
        [jax.ShapeDtypeStruct((width // rows, 2 * rows, 128), BF), pieces(4), pieces(4)],
        [
            pltpu.VMEM((8, 128, 128), BF),
            pltpu.VMEM((8, 128, 128), F32),
            pltpu.VMEM((3, 8, 128, 128), BF),
            pltpu.SemaphoreType.DMA((4,)),
        ],
    )
    terms = lax.all_to_all(terms, SEQ + ("rep",), 0, 0, tiled=True)
    got = across(send, HEAD, 1)
    pairs = small_call(pack_kernel, [keep, got], [pieces(2)] * 3)
    pairs = [across(pair, HEAD, 2 * k + 2) for k, pair in enumerate(pairs)]
    (d_inputs,) = products_call(
        inputs_kernel, (place,), (keep, got, *pairs, partial), weights, (1, 2),
        (BF,), [pltpu.VMEM((HEADS, BLOCK, 128), BF)],
    )
    (summed,) = small_call(
        gather_kernel, [terms],
        [jax.ShapeDtypeStruct((4, rows, HEADS * HEAD_DIM), F32)],
    )
    return (output[None], d_inputs[None], summed)


def solution(mesh):
    replicas = mesh.devices.shape[1]
    grid = Mesh(mesh.devices.reshape(4, 8, replicas), SEQ + ("rep",))
    return jax.shard_map(
        body,
        mesh=grid,
        in_specs=(
            P("rep", SEQ, None),
            P("rep", SEQ, None),
            P(),
            P("rep", None, None),
            P("rep", None),
        ),
        out_specs=(
            P("rep", SEQ, None),
            P("rep", SEQ, None),
            P(None, SEQ + ("rep",), None),
        ),
        check_vma=False,
    )
```

```python
import jax
import jax.numpy as jnp
from jax import lax
from jax.experimental import pallas as pl
from jax.experimental.pallas import tpu as pltpu
from jax.sharding import Mesh, PartitionSpec as P


HEADS = 8
HEAD_DIM = 64
BLOCK = 128
MAXN = 27
LARGE = 8
SLOTS = 28
BF = jnp.bfloat16
F32 = jnp.float32
INTERPRET = False


def dot(a, b):
    return jnp.dot(a, b, preferred_element_type=F32)


def dot_t(a, b):
    return lax.dot_general(a, b, (((1,), (1,)), ((), ())), preferred_element_type=F32)


def grant(mib):
    return pltpu.CompilerParams(vmem_limit_bytes=mib << 20)


def vmem(count):
    return [pl.BlockSpec(memory_space=pltpu.VMEM) for _ in range(count)]


def hbm(count):
    return [pl.BlockSpec(memory_space=pltpu.HBM) for _ in range(count)]


def position(high, low):
    return low * 8 + high


def by_head(rows, out_ref):
    for head in range(HEADS):
        cols = slice(head * HEAD_DIM, (head + 1) * HEAD_DIM)
        out_ref[head] = jnp.concatenate([rows[0, :, cols], rows[1, :, cols]], axis=1)


def keys_kernel(tok_ref, w_ref, kv_ref, rows):
    step = pl.program_id(0)
    rows[step] = dot(tok_ref[...], w_ref[0]).astype(BF)

    @pl.when(step == 1)
    def _():
        by_head(rows, kv_ref)


def queries_kernel(tok_ref, cot_ref, w_ref, qd_ref, xt_ref, rows):
    step = pl.program_id(0)

    @pl.when(step == 0)
    def _():
        queries = dot(tok_ref[...], w_ref[0]).astype(BF)
        rows[0] = (queries.astype(F32) * 0.125).astype(BF)
        xt_ref[0] = tok_ref[...].T

    @pl.when(step == 1)
    def _():
        rows[1] = dot(cot_ref[...], w_ref[0]).astype(BF)
        xt_ref[1] = cot_ref[...].T
        by_head(rows, qd_ref)


def project(kernel, arrays, weights, pick, outs):
    rows, width = arrays[0].shape
    columns = HEADS * HEAD_DIM
    return pl.pallas_call(
        kernel,
        grid=(2,),
        in_specs=[pl.BlockSpec((rows, width), lambda step: (0, 0)) for _ in arrays]
        + [pl.BlockSpec((1, width, columns), lambda step: (pick(step), 0, 0))],
        out_specs=[pl.BlockSpec(out, lambda step: (0, 0, 0)) for out in outs],
        out_shape=[jax.ShapeDtypeStruct(out, BF) for out in outs],
        scratch_shapes=[pltpu.VMEM((2, rows, columns), BF)],
        cost_estimate=pl.CostEstimate(
            flops=1_000_000_000, bytes_accessed=4_000_000, transcendentals=0
        ),
        compiler_params=grant(56),
        interpret=INTERPRET,
    )(*arrays, weights)


def attend_kernel(
    lists_ref, counts_ref, group_ref,
    qd_ref, kv0, kv1, kv2_low, kv2_high, kv3,
    y_ref, out0, out1, out2, out3,
    kvs, kvt, acc, s_scr, p_scr, ds_scr, n_scr, w_in, w_back, places, sems,
):
    step = pl.program_id(0)
    group = group_ref[0]
    block = position(step, group)

    @pl.when(step == 0)
    def _():
        copies = [
            pltpu.make_async_copy(ref, kvs.at[pl.ds(start, ref.shape[0])], sems.at[index])
            for index, (start, ref) in enumerate(
                ((0, kv0), (8, kv1), (16, kv2_low), (20, kv2_high), (24, kv3))
            )
        ]
        for copy in copies:
            copy.start()
        acc[...] = jnp.zeros_like(acc)
        for copy in copies:
            copy.wait()
        for idx in range(32):
            kvt[idx] = kvs[idx].T

    count = counts_ref[block]
    eights = (count + 1) // 8
    rest = count - eights * 8
    fours = (rest + 1) // 4
    twos = (rest - fours * 4 + 1) // 2

    def sweep(visit, carry):
        after = eights * 8
        carry = lax.fori_loop(0, eights, lambda i, c: visit(8, i * 8, c), carry)
        carry = lax.fori_loop(0, fours, lambda i, c: visit(4, after + i * 4, c), carry)
        after = after + fours * 4
        return lax.fori_loop(0, twos, lambda i, c: visit(2, after + i * 2, c), carry)

    def place(slot):
        raw = lists_ref[block, jnp.minimum(slot, MAXN - 1)]
        raw = jnp.where(slot < count, raw, block)
        where = raw ^ (group * 8)
        places[slot] = where
        return where

    qd = qd_ref[0]
    qdt = qd.T
    upper = lax.broadcasted_iota(jnp.int32, (128, 128), 0) < HEAD_DIM
    left = lax.broadcasted_iota(jnp.int32, (128, 128), 1) < HEAD_DIM
    zero = jnp.zeros((128, 128), BF)
    w_in[:, :128] = jnp.where(upper, qdt, zero)
    w_in[:, 128:] = jnp.where(upper, zero, qdt)
    w_back[:128] = jnp.where(left, qd, zero)
    w_back[128:] = jnp.where(left, zero, qd)

    def rows_of(slot, size):
        return pl.ds(pl.multiple_of(slot * 128, 128), size * 128)

    def scores(size, slot, top):
        stack = jnp.concatenate([kvs[place(slot + i)] for i in range(size)], axis=0)
        both = dot(stack, w_in[...])
        s_scr[rows_of(slot, size), :] = both[:, :128]
        p_scr[rows_of(slot, size), :] = both[:, 128:]
        return jnp.maximum(top, jnp.max(both[:, :128].reshape(size * 16, 8, 128), axis=0))

    top = sweep(scores, jnp.full((8, 128), -3e38, F32))
    row_max = jnp.max(top, axis=0, keepdims=True)

    def mix(size, slot, carry):
        total, mixed = carry
        parts, values = [], []
        for i in range(size):
            shift = jnp.where(slot + i < count, row_max, 1e30)
            e = jnp.exp(s_scr[rows_of(slot + i, 1), :] - shift)
            s_scr[rows_of(slot + i, 1), :] = e
            total = total + jnp.sum(e.reshape(16, 8, 128), axis=0)
            parts.append(e.astype(BF))
            values.append(kvt[places[slot + i], HEAD_DIM:, :])
        mixed = mixed + dot(jnp.concatenate(values, axis=1), jnp.concatenate(parts, axis=0))
        return total, mixed

    total, mixed = sweep(mix, (jnp.zeros((8, 128), F32), jnp.zeros((HEAD_DIM, 128), F32)))
    inverse = 1.0 / jnp.sum(total, axis=0, keepdims=True)
    attended = (mixed * inverse).astype(BF)
    delta = jnp.sum(
        qdt[HEAD_DIM:, :].astype(F32) * attended.astype(F32), axis=0, keepdims=True
    )

    def back(size, slot, dq):
        keys = []
        for i in range(size):
            rows, here = rows_of(slot + i, 1), slice(i * 128, (i + 1) * 128)
            normed = s_scr[rows, :] * inverse
            ds_scr[here, :] = (normed * (p_scr[rows, :] - delta)).astype(BF)
            n_scr[here, :] = normed.astype(BF)
            keys.append(kvt[places[slot + i], :HEAD_DIM, :])
        span = slice(0, size * 128)
        dq = dq + dot(jnp.concatenate(keys, axis=1), ds_scr[span, :])
        grads = dot(jnp.concatenate([ds_scr[span, :], n_scr[span, :]], axis=1), w_back[...])
        for i in range(size):
            acc[places[slot + i]] += grads[i * 128 : (i + 1) * 128]
        return dq

    dq = sweep(back, jnp.zeros((HEAD_DIM, 128), F32))
    y_ref[0] = jnp.concatenate([dq * 0.125, attended.astype(F32)], axis=0).T.astype(BF)

    @pl.when(step == 7)
    def _():
        for part, ref in enumerate((out0, out1, out2, out3)):
            for idx in range(8):
                ref[idx] = acc[8 * part + idx].astype(ref.dtype)


def attend(lists, counts, group, qd, kvs):
    whole3 = lambda step, *_: (0, 0, 0)
    piece = pl.BlockSpec((8, 128, 128), whole3)
    each = pl.BlockSpec((1, 128, 128), lambda step, *_: (step, 0, 0))
    shape = lambda dtype: jax.ShapeDtypeStruct((8, 128, 128), dtype)
    return pl.pallas_call(
        attend_kernel,
        grid_spec=pltpu.PrefetchScalarGridSpec(
            num_scalar_prefetch=3,
            grid=(8,),
            in_specs=[each] + hbm(5),
            out_specs=[each] + [piece] * 4,
            scratch_shapes=[
                pltpu.VMEM((32, 128, 128), BF),
                pltpu.VMEM((32, 128, 128), BF),
                pltpu.VMEM((32, 128, 128), F32),
                pltpu.VMEM((SLOTS * 128, 128), F32),
                pltpu.VMEM((SLOTS * 128, 128), F32),
                pltpu.VMEM((LARGE * 128, 128), BF),
                pltpu.VMEM((LARGE * 128, 128), BF),
                pltpu.VMEM((128, 256), BF),
                pltpu.VMEM((256, 128), BF),
                pltpu.SMEM((SLOTS,), jnp.int32),
                pltpu.SemaphoreType.DMA((5,)),
            ],
        ),
        out_shape=[shape(BF), shape(F32), shape(BF), shape(BF), shape(BF)],
        cost_estimate=pl.CostEstimate(
            flops=30_000_000_000, bytes_accessed=4_000_000, transcendentals=4_000_000
        ),
        compiler_params=grant(28),
        interpret=INTERPRET,
        name="attend",
    )(lists, counts, group, qd, *kvs)


def ordered(y_ref, place):
    return jnp.concatenate([y_ref[place ^ k] for k in (0, 2, 4, 6, 1, 3, 5, 7)], axis=0)


def first_grads_kernel(place_ref, y_ref, *refs):
    xs, out_ref = refs[:8], refs[8]
    y = ordered(y_ref, place_ref[0])
    tok = dot(jnp.concatenate([x[0] for x in xs], axis=1), y)
    cot = dot(jnp.concatenate([x[1] for x in xs], axis=1), y)
    left = lax.broadcasted_iota(jnp.int32, tok.shape, 1) < HEAD_DIM
    out_ref[...] = jnp.where(left, tok, cot)


def second_grads_kernel(place_ref, own, part1, part2, part3, first_ref, *refs):
    xs, (out_ref, keep_ref, send_ref, y_ref, base, landed, sems) = refs[:8], refs[8:]
    copies = [pltpu.make_async_copy(own, base, sems.at[0])] + [
        pltpu.make_async_copy(part, landed.at[k], sems.at[k + 1])
        for k, part in enumerate((part1, part2, part3))
    ]
    for copy in copies:
        copy.start()
    for copy in copies:
        copy.wait()
    y_ref[...] = (base[...] + jnp.sum(landed[...].astype(F32), axis=0)).astype(BF)
    chip, core = place_ref[0] // 2, lax.rem(place_ref[0], 2)
    for k in range(4):
        keep_ref[k] = y_ref[(chip ^ k) * 2 + core]
        send_ref[k] = y_ref[(chip ^ k) * 2 + 1 - core]
    y = ordered(y_ref, place_ref[0])
    second = dot(jnp.concatenate([x[0] for x in xs], axis=1), y)
    rows = out_ref.shape[1] // 2
    for index in range(out_ref.shape[0]):
        mine = slice(index * rows, (index + 1) * rows)
        out_ref[index] = jnp.concatenate([first_ref[mine], second[mine]], axis=0).astype(BF)


def pack_kernel(keep_ref, got_ref, *outs):
    for k, ref in enumerate(outs):
        ref[0] = keep_ref[k + 1]
        ref[1] = got_ref[k + 1]


def grads_call(kernel, place, specs, operands, outs, scratch=()):
    return pl.pallas_call(
        kernel,
        in_specs=[pl.BlockSpec(memory_space=pltpu.SMEM)] + specs,
        out_specs=vmem(len(outs)),
        out_shape=outs,
        scratch_shapes=list(scratch),
        cost_estimate=pl.CostEstimate(
            flops=2_000_000_000, bytes_accessed=4_000_000, transcendentals=0
        ),
        compiler_params=grant(16),
        interpret=INTERPRET,
    )(place, *operands)


def gather_kernel(in_ref, out_ref):
    replicas, rows = in_ref.shape[0] // 32, in_ref.shape[1] // 2
    parts = []
    for head in range(HEADS):
        total = None
        for low in range(4):
            start = position(head, low) * replicas
            term = jnp.sum(in_ref[start : start + replicas].astype(F32), axis=0)
            total = term if total is None else total + term
        parts.append(total)
    for half, (near, far) in enumerate(((0, 3), (1, 2))):
        mine = slice(half * rows, (half + 1) * rows)
        out_ref[near] = jnp.concatenate([p[mine, :HEAD_DIM] for p in parts], axis=1)
        out_ref[far] = jnp.concatenate([p[mine, HEAD_DIM:] for p in parts], axis=1)


def small_call(kernel, operands, outs):
    return pl.pallas_call(
        kernel,
        in_specs=vmem(len(operands)),
        out_specs=vmem(len(outs)),
        out_shape=outs,
        compiler_params=grant(4),
        interpret=INTERPRET,
    )(*operands)


def halves(pieces):
    first = jnp.concatenate([piece[:, :HEAD_DIM] for piece in pieces], axis=1)
    second = jnp.concatenate([piece[:, HEAD_DIM:] for piece in pieces], axis=1)
    return first, second


def output_kernel(y_ref, wq_ref, wo_ref, out_ref, part_ref):
    dq, attended = halves([y_ref[head] for head in range(HEADS)])
    out_ref[...] = dot_t(attended, wo_ref[0]).astype(BF)
    part_ref[...] = dot_t(dq, wq_ref[0])


def inputs_kernel(place_ref, keep_ref, got_ref, *refs):
    pairs, (part_ref, wk_ref, wv_ref, out_ref, heads) = refs[:3], refs[3:]
    place = place_ref[0]
    heads[place] = keep_ref[0]
    heads[place ^ 1] = got_ref[0]
    for k, pair in enumerate(pairs):
        heads[place ^ (2 * k + 2)] = pair[0]
        heads[place ^ (2 * k + 3)] = pair[1]
    dk, dv = halves([heads[head] for head in range(HEADS)])
    out_ref[...] = (part_ref[...] + dot_t(dk, wk_ref[0]) + dot_t(dv, wv_ref[0])).astype(BF)


def products_call(kernel, place, arrays, weights, picks, outs, scratch=()):
    whole = lambda array: pl.BlockSpec(array.shape, lambda step: (0,) * array.ndim)
    width = weights.shape[1]
    pick = lambda m: pl.BlockSpec((1, width, HEADS * HEAD_DIM), lambda step: (m, 0, 0))
    return pl.pallas_call(
        kernel,
        grid=(1,),
        in_specs=[pl.BlockSpec(memory_space=pltpu.SMEM) for _ in place]
        + [whole(array) for array in arrays]
        + [pick(m) for m in picks],
        out_specs=[pl.BlockSpec((BLOCK, width), lambda step: (0, 0)) for _ in outs],
        out_shape=[jax.ShapeDtypeStruct((BLOCK, width), dtype) for dtype in outs],
        scratch_shapes=list(scratch),
        cost_estimate=pl.CostEstimate(
            flops=500_000_000, bytes_accessed=4_000_000, transcendentals=0
        ),
        compiler_params=grant(12),
        interpret=INTERPRET,
    )(*place, *arrays, *[weights for _ in picks])


ROW = ("row",)
HEAD = ("head",)
SEQ = ROW + HEAD


def across(array, axes, flip):
    return lax.ppermute(array, axes, [(i, i ^ flip) for i in range(lax.axis_size(axes))])


def body(tokens, cotangent, weights, neighbour_lists, neighbour_counts):
    width = tokens.shape[2]
    rows = width // (32 * lax.axis_size("rep"))
    group = lax.axis_index(ROW).astype(jnp.int32).reshape(1)
    place = lax.axis_index(HEAD).astype(jnp.int32).reshape(1)
    swap = lambda array: lax.all_to_all(array, HEAD, 0, 0, tiled=True)
    (kv,) = project(
        keys_kernel, [tokens[0]], weights, lambda step: step + 1,
        [(HEADS, BLOCK, 128)],
    )
    kv = swap(kv)
    qd, xt = project(
        queries_kernel, [tokens[0], cotangent[0]], weights,
        lambda step: 3 * step, [(HEADS, BLOCK, 128), (2, width, BLOCK)],
    )
    qd, xt, kv = lax.optimization_barrier((qd, xt, kv))
    one, three = across(kv, ROW, 1), across(kv, ROW, 3)
    low, high = across(one[:4], ROW, 3), across(three[4:], ROW, 1)
    kvs = [kv, one, low, high, three]
    qd = swap(qd)
    xs = [xt] + [across(xt, HEAD, k) for k in (2, 4, 6)]
    y, *parts = attend(neighbour_lists[0], neighbour_counts[0], group, qd, kvs)
    xs, y = lax.optimization_barrier((xs, y))
    xs = xs + [across(x, HEAD, 1) for x in xs]
    parts = [parts[0]] + [across(parts[k], ROW, k) for k in (1, 2, 3)]
    home = swap(y)
    (first,) = grads_call(
        first_grads_kernel, place, vmem(9), [y, *xs],
        [jax.ShapeDtypeStruct((width, 128), F32)],
    )
    output, partial = products_call(output_kernel, (), (home,), weights, (0, 3), (BF, F32))
    pieces = lambda count: jax.ShapeDtypeStruct((count, 128, 128), BF)
    terms, keep, send = grads_call(
        second_grads_kernel, place, hbm(4) + vmem(9),
        [*parts, first, *xs],
        [jax.ShapeDtypeStruct((width // rows, 2 * rows, 128), BF), pieces(4), pieces(4)],
        [
            pltpu.VMEM((8, 128, 128), BF),
            pltpu.VMEM((8, 128, 128), F32),
            pltpu.VMEM((3, 8, 128, 128), BF),
            pltpu.SemaphoreType.DMA((4,)),
        ],
    )
    terms = lax.all_to_all(terms, SEQ + ("rep",), 0, 0, tiled=True)
    got = across(send, HEAD, 1)
    pairs = small_call(pack_kernel, [keep, got], [pieces(2)] * 3)
    pairs = [across(pair, HEAD, 2 * k + 2) for k, pair in enumerate(pairs)]
    (d_inputs,) = products_call(
        inputs_kernel, (place,), (keep, got, *pairs, partial), weights, (1, 2),
        (BF,), [pltpu.VMEM((HEADS, BLOCK, 128), BF)],
    )
    (summed,) = small_call(
        gather_kernel, [terms],
        [jax.ShapeDtypeStruct((4, rows, HEADS * HEAD_DIM), F32)],
    )
    return (output[None], d_inputs[None], summed)


def solution(mesh):
    replicas = mesh.devices.shape[1]
    grid = Mesh(mesh.devices.reshape(4, 8, replicas), SEQ + ("rep",))
    return jax.shard_map(
        body,
        mesh=grid,
        in_specs=(
            P("rep", SEQ, None),
            P("rep", SEQ, None),
            P(),
            P("rep", None, None),
            P("rep", None),
        ),
        out_specs=(
            P("rep", SEQ, None),
            P("rep", SEQ, None),
            P(None, SEQ + ("rep",), None),
        ),
        check_vma=False,
    )
```

```python
import jax
import jax.numpy as jnp
from jax import lax
from jax.experimental import pallas as pl
from jax.experimental.pallas import tpu as pltpu
from jax.sharding import Mesh, PartitionSpec as P


HEADS = 8
HEAD_DIM = 64
BLOCK = 128
MAXN = 27
LARGE = 8
SLOTS = 28
BF = jnp.bfloat16
F32 = jnp.float32
INTERPRET = False


def dot(a, b):
    return jnp.dot(a, b, preferred_element_type=F32)


def dot_t(a, b):
    return lax.dot_general(a, b, (((1,), (1,)), ((), ())), preferred_element_type=F32)


def grant(mib):
    return pltpu.CompilerParams(vmem_limit_bytes=mib << 20)


def vmem(count):
    return [pl.BlockSpec(memory_space=pltpu.VMEM) for _ in range(count)]


def hbm(count):
    return [pl.BlockSpec(memory_space=pltpu.HBM) for _ in range(count)]


def position(high, low):
    return low * 8 + high


def by_head(rows, out_ref):
    for head in range(HEADS):
        cols = slice(head * HEAD_DIM, (head + 1) * HEAD_DIM)
        out_ref[head] = jnp.concatenate([rows[0, :, cols], rows[1, :, cols]], axis=1)


def keys_kernel(tok_ref, w_ref, kv_ref, rows):
    step = pl.program_id(0)
    rows[step] = dot(tok_ref[...], w_ref[0]).astype(BF)

    @pl.when(step == 1)
    def _():
        by_head(rows, kv_ref)


def queries_kernel(tok_ref, cot_ref, w_ref, qd_ref, xt_ref, rows):
    step = pl.program_id(0)

    @pl.when(step == 0)
    def _():
        queries = dot(tok_ref[...], w_ref[0]).astype(BF)
        rows[0] = (queries.astype(F32) * 0.125).astype(BF)
        xt_ref[0] = tok_ref[...].T

    @pl.when(step == 1)
    def _():
        rows[1] = dot(cot_ref[...], w_ref[0]).astype(BF)
        xt_ref[1] = cot_ref[...].T
        by_head(rows, qd_ref)


def project(kernel, arrays, weights, pick, outs):
    rows, width = arrays[0].shape
    columns = HEADS * HEAD_DIM
    return pl.pallas_call(
        kernel,
        grid=(2,),
        in_specs=[pl.BlockSpec((rows, width), lambda step: (0, 0)) for _ in arrays]
        + [pl.BlockSpec((1, width, columns), lambda step: (pick(step), 0, 0))],
        out_specs=[pl.BlockSpec(out, lambda step: (0, 0, 0)) for out in outs],
        out_shape=[jax.ShapeDtypeStruct(out, BF) for out in outs],
        scratch_shapes=[pltpu.VMEM((2, rows, columns), BF)],
        cost_estimate=pl.CostEstimate(
            flops=1_000_000_000, bytes_accessed=4_000_000, transcendentals=0
        ),
        compiler_params=grant(56),
        interpret=INTERPRET,
    )(*arrays, weights)


def attend_kernel(
    lists_ref, counts_ref, group_ref,
    qd_ref, kv0, kv1, kv2, kv3,
    y_ref, out0, out1, out2, out3,
    kvs, kvt, acc, s_scr, p_scr, ds_scr, n_scr, w_in, w_back, places, sems,
):
    step = pl.program_id(0)
    group = group_ref[0]
    block = position(step, group)

    @pl.when(step == 0)
    def _():
        copies = [
            pltpu.make_async_copy(ref, kvs.at[pl.ds(8 * part, 8)], sems.at[part])
            for part, ref in enumerate((kv0, kv1, kv2, kv3))
        ]
        for copy in copies:
            copy.start()
        acc[...] = jnp.zeros_like(acc)
        for part, copy in enumerate(copies):
            copy.wait()
            for idx in range(8 * part, 8 * part + 8):
                kvt[idx] = kvs[idx].T

    count = counts_ref[block]
    eights = (count + 1) // 8
    rest = count - eights * 8
    fours = (rest + 1) // 4
    twos = (rest - fours * 4 + 1) // 2

    def sweep(visit, carry):
        after = eights * 8
        carry = lax.fori_loop(0, eights, lambda i, c: visit(8, i * 8, c), carry)
        carry = lax.fori_loop(0, fours, lambda i, c: visit(4, after + i * 4, c), carry)
        after = after + fours * 4
        return lax.fori_loop(0, twos, lambda i, c: visit(2, after + i * 2, c), carry)

    def place(slot):
        raw = lists_ref[block, jnp.minimum(slot, MAXN - 1)]
        raw = jnp.where(slot < count, raw, block)
        where = raw ^ (group * 8)
        places[slot] = where
        return where

    qd = qd_ref[0]
    qdt = qd.T
    upper = lax.broadcasted_iota(jnp.int32, (128, 128), 0) < HEAD_DIM
    left = lax.broadcasted_iota(jnp.int32, (128, 128), 1) < HEAD_DIM
    zero = jnp.zeros((128, 128), BF)
    w_in[:, :128] = jnp.where(upper, qdt, zero)
    w_in[:, 128:] = jnp.where(upper, zero, qdt)
    w_back[:128] = jnp.where(left, qd, zero)
    w_back[128:] = jnp.where(left, zero, qd)

    def rows_of(slot, size):
        return pl.ds(pl.multiple_of(slot * 128, 128), size * 128)

    def scores(size, slot, top):
        stack = jnp.concatenate([kvs[place(slot + i)] for i in range(size)], axis=0)
        both = dot(stack, w_in[...])
        s_scr[rows_of(slot, size), :] = both[:, :128]
        p_scr[rows_of(slot, size), :] = both[:, 128:]
        return jnp.maximum(top, jnp.max(both[:, :128].reshape(size * 16, 8, 128), axis=0))

    top = sweep(scores, jnp.full((8, 128), -3e38, F32))
    row_max = jnp.max(top, axis=0, keepdims=True)

    def mix(size, slot, carry):
        total, mixed = carry
        parts, values = [], []
        for i in range(size):
            shift = jnp.where(slot + i < count, row_max, 1e30)
            e = jnp.exp(s_scr[rows_of(slot + i, 1), :] - shift)
            s_scr[rows_of(slot + i, 1), :] = e
            total = total + jnp.sum(e.reshape(16, 8, 128), axis=0)
            parts.append(e.astype(BF))
            values.append(kvt[places[slot + i], HEAD_DIM:, :])
        mixed = mixed + dot(jnp.concatenate(values, axis=1), jnp.concatenate(parts, axis=0))
        return total, mixed

    total, mixed = sweep(mix, (jnp.zeros((8, 128), F32), jnp.zeros((HEAD_DIM, 128), F32)))
    inverse = 1.0 / jnp.sum(total, axis=0, keepdims=True)
    attended = (mixed * inverse).astype(BF)
    delta = jnp.sum(
        qdt[HEAD_DIM:, :].astype(F32) * attended.astype(F32), axis=0, keepdims=True
    )

    def back(size, slot, dq):
        keys = []
        for i in range(size):
            rows, here = rows_of(slot + i, 1), slice(i * 128, (i + 1) * 128)
            normed = s_scr[rows, :] * inverse
            ds_scr[here, :] = (normed * (p_scr[rows, :] - delta)).astype(BF)
            n_scr[here, :] = normed.astype(BF)
            keys.append(kvt[places[slot + i], :HEAD_DIM, :])
        span = slice(0, size * 128)
        dq = dq + dot(jnp.concatenate(keys, axis=1), ds_scr[span, :])
        grads = dot(jnp.concatenate([ds_scr[span, :], n_scr[span, :]], axis=1), w_back[...])
        for i in range(size):
            acc[places[slot + i]] += grads[i * 128 : (i + 1) * 128]
        return dq

    dq = sweep(back, jnp.zeros((HEAD_DIM, 128), F32))
    y_ref[0] = jnp.concatenate([dq * 0.125, attended.astype(F32)], axis=0).T.astype(BF)

    @pl.when(step == 7)
    def _():
        for part, ref in enumerate((out0, out1, out2, out3)):
            for idx in range(8):
                ref[idx] = acc[8 * part + idx].astype(ref.dtype)


def attend(lists, counts, group, qd, kvs):
    whole3 = lambda step, *_: (0, 0, 0)
    piece = pl.BlockSpec((8, 128, 128), whole3)
    each = pl.BlockSpec((1, 128, 128), lambda step, *_: (step, 0, 0))
    shape = lambda dtype: jax.ShapeDtypeStruct((8, 128, 128), dtype)
    return pl.pallas_call(
        attend_kernel,
        grid_spec=pltpu.PrefetchScalarGridSpec(
            num_scalar_prefetch=3,
            grid=(8,),
            in_specs=[each] + hbm(4),
            out_specs=[each] + [piece] * 4,
            scratch_shapes=[
                pltpu.VMEM((32, 128, 128), BF),
                pltpu.VMEM((32, 128, 128), BF),
                pltpu.VMEM((32, 128, 128), F32),
                pltpu.VMEM((SLOTS * 128, 128), F32),
                pltpu.VMEM((SLOTS * 128, 128), F32),
                pltpu.VMEM((LARGE * 128, 128), BF),
                pltpu.VMEM((LARGE * 128, 128), BF),
                pltpu.VMEM((128, 256), BF),
                pltpu.VMEM((256, 128), BF),
                pltpu.SMEM((SLOTS,), jnp.int32),
                pltpu.SemaphoreType.DMA((4,)),
            ],
        ),
        out_shape=[shape(BF), shape(F32), shape(BF), shape(BF), shape(BF)],
        cost_estimate=pl.CostEstimate(
            flops=30_000_000_000, bytes_accessed=4_000_000, transcendentals=4_000_000
        ),
        compiler_params=grant(28),
        interpret=INTERPRET,
        name="attend",
    )(lists, counts, group, qd, *kvs)


def ordered(y_ref, place):
    return jnp.concatenate([y_ref[place ^ k] for k in (0, 2, 4, 6, 1, 3, 5, 7)], axis=0)


def first_grads_kernel(place_ref, y_ref, *refs):
    xs, out_ref = refs[:8], refs[8]
    y = ordered(y_ref, place_ref[0])
    tok = dot(jnp.concatenate([x[0] for x in xs], axis=1), y)
    cot = dot(jnp.concatenate([x[1] for x in xs], axis=1), y)
    left = lax.broadcasted_iota(jnp.int32, tok.shape, 1) < HEAD_DIM
    out_ref[...] = jnp.where(left, tok, cot)


def second_grads_kernel(place_ref, own, part1, part2, part3, first_ref, *refs):
    xs, (out_ref, keep_ref, send_ref, y_ref, base, landed, sems) = refs[:8], refs[8:]
    copies = [pltpu.make_async_copy(own, base, sems.at[0])] + [
        pltpu.make_async_copy(part, landed.at[k], sems.at[k + 1])
        for k, part in enumerate((part1, part2, part3))
    ]
    for copy in copies:
        copy.start()
    for copy in copies:
        copy.wait()
    y_ref[...] = (base[...] + jnp.sum(landed[...].astype(F32), axis=0)).astype(BF)
    chip, core = place_ref[0] // 2, lax.rem(place_ref[0], 2)
    for k in range(4):
        keep_ref[k] = y_ref[(chip ^ k) * 2 + core]
        send_ref[k] = y_ref[(chip ^ k) * 2 + 1 - core]
    y = ordered(y_ref, place_ref[0])
    second = dot(jnp.concatenate([x[0] for x in xs], axis=1), y)
    rows = out_ref.shape[1] // 2
    for index in range(out_ref.shape[0]):
        mine = slice(index * rows, (index + 1) * rows)
        out_ref[index] = jnp.concatenate([first_ref[mine], second[mine]], axis=0).astype(BF)


def pack_kernel(keep_ref, got_ref, *outs):
    for k, ref in enumerate(outs):
        ref[0] = keep_ref[k + 1]
        ref[1] = got_ref[k + 1]


def grads_call(kernel, place, specs, operands, outs, scratch=()):
    return pl.pallas_call(
        kernel,
        in_specs=[pl.BlockSpec(memory_space=pltpu.SMEM)] + specs,
        out_specs=vmem(len(outs)),
        out_shape=outs,
        scratch_shapes=list(scratch),
        cost_estimate=pl.CostEstimate(
            flops=2_000_000_000, bytes_accessed=4_000_000, transcendentals=0
        ),
        compiler_params=grant(16),
        interpret=INTERPRET,
    )(place, *operands)


def gather_kernel(in_ref, out_ref):
    replicas, rows = in_ref.shape[0] // 32, in_ref.shape[1] // 2
    parts = []
    for head in range(HEADS):
        total = None
        for low in range(4):
            start = position(head, low) * replicas
            term = jnp.sum(in_ref[start : start + replicas].astype(F32), axis=0)
            total = term if total is None else total + term
        parts.append(total)
    for half, (near, far) in enumerate(((0, 3), (1, 2))):
        mine = slice(half * rows, (half + 1) * rows)
        out_ref[near] = jnp.concatenate([p[mine, :HEAD_DIM] for p in parts], axis=1)
        out_ref[far] = jnp.concatenate([p[mine, HEAD_DIM:] for p in parts], axis=1)


def small_call(kernel, operands, outs):
    return pl.pallas_call(
        kernel,
        in_specs=vmem(len(operands)),
        out_specs=vmem(len(outs)),
        out_shape=outs,
        compiler_params=grant(4),
        interpret=INTERPRET,
    )(*operands)


def halves(pieces):
    first = jnp.concatenate([piece[:, :HEAD_DIM] for piece in pieces], axis=1)
    second = jnp.concatenate([piece[:, HEAD_DIM:] for piece in pieces], axis=1)
    return first, second


def output_kernel(y_ref, wq_ref, wo_ref, out_ref, part_ref):
    dq, attended = halves([y_ref[head] for head in range(HEADS)])
    out_ref[...] = dot_t(attended, wo_ref[0]).astype(BF)
    part_ref[...] = dot_t(dq, wq_ref[0])


def inputs_kernel(place_ref, keep_ref, got_ref, *refs):
    pairs, (part_ref, wk_ref, wv_ref, out_ref, heads) = refs[:3], refs[3:]
    place = place_ref[0]
    heads[place] = keep_ref[0]
    heads[place ^ 1] = got_ref[0]
    for k, pair in enumerate(pairs):
        heads[place ^ (2 * k + 2)] = pair[0]
        heads[place ^ (2 * k + 3)] = pair[1]
    dk, dv = halves([heads[head] for head in range(HEADS)])
    out_ref[...] = (part_ref[...] + dot_t(dk, wk_ref[0]) + dot_t(dv, wv_ref[0])).astype(BF)


def products_call(kernel, place, arrays, weights, picks, outs, scratch=()):
    whole = lambda array: pl.BlockSpec(array.shape, lambda step: (0,) * array.ndim)
    width = weights.shape[1]
    pick = lambda m: pl.BlockSpec((1, width, HEADS * HEAD_DIM), lambda step: (m, 0, 0))
    return pl.pallas_call(
        kernel,
        grid=(1,),
        in_specs=[pl.BlockSpec(memory_space=pltpu.SMEM) for _ in place]
        + [whole(array) for array in arrays]
        + [pick(m) for m in picks],
        out_specs=[pl.BlockSpec((BLOCK, width), lambda step: (0, 0)) for _ in outs],
        out_shape=[jax.ShapeDtypeStruct((BLOCK, width), dtype) for dtype in outs],
        scratch_shapes=list(scratch),
        cost_estimate=pl.CostEstimate(
            flops=500_000_000, bytes_accessed=4_000_000, transcendentals=0
        ),
        compiler_params=grant(12),
        interpret=INTERPRET,
    )(*place, *arrays, *[weights for _ in picks])


ROW = ("row",)
HEAD = ("head",)
SEQ = ROW + HEAD


def across(array, axes, flip):
    return lax.ppermute(array, axes, [(i, i ^ flip) for i in range(lax.axis_size(axes))])


def body(tokens, cotangent, weights, neighbour_lists, neighbour_counts):
    width = tokens.shape[2]
    rows = width // (32 * lax.axis_size("rep"))
    group = lax.axis_index(ROW).astype(jnp.int32).reshape(1)
    place = lax.axis_index(HEAD).astype(jnp.int32).reshape(1)
    swap = lambda array: lax.all_to_all(array, HEAD, 0, 0, tiled=True)
    (kv,) = project(
        keys_kernel, [tokens[0]], weights, lambda step: step + 1,
        [(HEADS, BLOCK, 128)],
    )
    kv = swap(kv)
    qd, xt = project(
        queries_kernel, [tokens[0], cotangent[0]], weights,
        lambda step: 3 * step, [(HEADS, BLOCK, 128), (2, width, BLOCK)],
    )
    qd, xt, kv = lax.optimization_barrier((qd, xt, kv))
    kvs = [kv] + [across(kv, ROW, k) for k in (1, 2, 3)]
    qd = swap(qd)
    xs = [xt] + [across(xt, HEAD, k) for k in (2, 4, 6)]
    y, *parts = attend(neighbour_lists[0], neighbour_counts[0], group, qd, kvs)
    xs, y = lax.optimization_barrier((xs, y))
    xs = xs + [across(x, HEAD, 1) for x in xs]
    parts = [parts[0]] + [across(parts[k], ROW, k) for k in (1, 2, 3)]
    home = swap(y)
    (first,) = grads_call(
        first_grads_kernel, place, vmem(9), [y, *xs],
        [jax.ShapeDtypeStruct((width, 128), F32)],
    )
    output, partial = products_call(output_kernel, (), (home,), weights, (0, 3), (BF, F32))
    pieces = lambda count: jax.ShapeDtypeStruct((count, 128, 128), BF)
    terms, keep, send = grads_call(
        second_grads_kernel, place, hbm(4) + vmem(9),
        [*parts, first, *xs],
        [jax.ShapeDtypeStruct((width // rows, 2 * rows, 128), BF), pieces(4), pieces(4)],
        [
            pltpu.VMEM((8, 128, 128), BF),
            pltpu.VMEM((8, 128, 128), F32),
            pltpu.VMEM((3, 8, 128, 128), BF),
            pltpu.SemaphoreType.DMA((4,)),
        ],
    )
    terms = lax.all_to_all(terms, SEQ + ("rep",), 0, 0, tiled=True)
    got = across(send, HEAD, 1)
    pairs = small_call(pack_kernel, [keep, got], [pieces(2)] * 3)
    pairs = [across(pair, HEAD, 2 * k + 2) for k, pair in enumerate(pairs)]
    (d_inputs,) = products_call(
        inputs_kernel, (place,), (keep, got, *pairs, partial), weights, (1, 2),
        (BF,), [pltpu.VMEM((HEADS, BLOCK, 128), BF)],
    )
    (summed,) = small_call(
        gather_kernel, [terms],
        [jax.ShapeDtypeStruct((4, rows, HEADS * HEAD_DIM), F32)],
    )
    return (output[None], d_inputs[None], summed)


def solution(mesh):
    replicas = mesh.devices.shape[1]
    grid = Mesh(mesh.devices.reshape(4, 8, replicas), SEQ + ("rep",))
    return jax.shard_map(
        body,
        mesh=grid,
        in_specs=(
            P("rep", SEQ, None),
            P("rep", SEQ, None),
            P(),
            P("rep", None, None),
            P("rep", None),
        ),
        out_specs=(
            P("rep", SEQ, None),
            P("rep", SEQ, None),
            P(None, SEQ + ("rep",), None),
        ),
        check_vma=False,
    )
```
